32 devices in a mesh: section: 4 (over y, x), dp: 8 (over z, core).
Axes of the slice: x: 2, y: 2, z: 4, core: 2. Of those that a mesh axis runs over, the one named last changes fastest.
Arguments:
- acts: bfloat16 [4, 2048, 2560], P('section', 'dp'), may hold values from -6 to 6
- gates: bfloat16 [4, 2048, 1280], P('section', 'dp'), may hold values from -6 to 6
- w_value: bfloat16 [4, 2560, 1280], P('section', 'dp'), may hold values from -0.125 to 0.125
- w_out: bfloat16 [4, 2560, 1280], P('section', 'dp'), may hold values from -0.125 to 0.125
- residual_error: bfloat16 [4, 20480, 1280], P('section', 'dp'), may hold values from -48 to 48
- grad_top: bfloat16 [2048, 2560], P('dp'), may hold values from -6 to 6
- warm_factor: float32 [4, 4, 1280], P('section'), may hold values from -6 to 6
Outputs:
- grad_in: bfloat16 [4, 2048, 2560], P('section', 'dp')
- basis_out: float32 [4, 4, 2560], P('section')
- right_out: float32 [4, 4, 1280], P('section')
The draws below stay inside these ranges and needn't reach their ends.
All inputs are finite; a program needn't handle non-finite values.
Results may differ from the reference program's by a relative error of at most 0.009.
Values may be sent and summed in bfloat16 or wider, within the bound.
No kernel may reach another device: no remote copies, remote signals or barrier semaphores. Data moves between devices by JAX's collectives and lax.ppermute only.
A program may use at most 128 MiB of HBM per device.

```python
import math
import jax
import jax.numpy as jnp
from jax import lax

D = 2560
C = 1280
RANK = 4
TOKENS = 2048
N_SECTION = 4
N_DP = 8


def steps_of(key, extent, pieces, least, largest):
    def one(dim, parts):
        steps = jax.random.uniform(jax.random.fold_in(jax.random.fold_in(key, 6), dim), (parts,), jnp.float32, least / len(pieces), largest / len(pieces))
        return jnp.repeat(jnp.exp(steps), extent[dim] // parts).reshape((-1,) + (1,) * (len(extent) - dim - 1))

    gain = one(*pieces[0])
    for cut in pieces[1:]:
        gain = gain * one(*cut)
    return gain


def bell_draw(key, shape, spread, most, shards=(), held_as=jnp.bfloat16):
    array = spread * jax.random.normal(key, shape, jnp.float32)
    if shards:
        array = array * steps_of(key, shape, shards, -0.22, 0.18)
    return jnp.clip(array, -most, most).astype(held_as)


def setup_inputs(seed: int = 0) -> dict:
    arg_keys = jax.random.split(jax.random.key(seed), 8)
    return {
        "acts": bell_draw(arg_keys[0], (N_SECTION, TOKENS, D), 1.0, 6.0, ((0, 4), (1, 8))),
        "gates": bell_draw(arg_keys[1], (N_SECTION, TOKENS, C), 1.0, 6.0, ((0, 4), (1, 8))),
        "w_value": bell_draw(arg_keys[2], (N_SECTION, D, C), D ** -0.5, 0.125, ((0, 4), (1, 8))),
        "w_out": bell_draw(arg_keys[3], (N_SECTION, D, C), D ** -0.5, 0.125, ((0, 4), (1, 8))),
        "residual_error": bell_draw(arg_keys[4], (N_SECTION, N_DP * D, C), 8.0, 48.0, ((0, 4), (1, 8))),
        "grad_top": bell_draw(arg_keys[5], (TOKENS, D), 1.0, 6.0, ((0, 8),)),
        "warm_factor": bell_draw(arg_keys[6], (N_SECTION, RANK, C), 1.0, 6.0, ((0, 4),), jnp.float32),
    }


HIGHEST_PRECISION = lax.Precision.HIGHEST

def orthonormal(vectors):
    result = []
    for column in range(vectors.shape[0]):
        current = vectors[column]
        for previous in result:
            current = current - jnp.mean(current * previous) * previous
        current = current / jnp.sqrt(jnp.mean(current * current) + 1e-06)
        result.append(current)
    return jnp.stack(result)

def reference(acts, gates, w_value, w_out, residual_error, grad_top, warm_factor):
    arriving = grad_top
    passed_list = []
    basis_list = []
    right_list = []
    for layer_index in reversed(range(N_SECTION)):
        hidden = jnp.dot(arriving, w_out[layer_index], preferred_element_type=jnp.float32)
        value_grad = (hidden * gates[layer_index].astype(jnp.float32)).astype(jnp.bfloat16)
        back_term = lax.dot_general(value_grad, w_value[layer_index], (((1,), (1,)), ((), ())), preferred_element_type=jnp.float32)
        passed = (arriving.astype(jnp.float32) + back_term).astype(jnp.bfloat16)
        inputs_wide = acts[layer_index].astype(jnp.float32)
        grads_wide = value_grad.astype(jnp.float32)
        error_sum = lax.optimization_barrier(jnp.sum(residual_error[layer_index].astype(jnp.float32).reshape(N_DP, D, C), axis=0))
        warm_start = warm_factor[layer_index]
        projected = jnp.dot(grads_wide, warm_start.T, precision=HIGHEST_PRECISION)
        factor = jnp.dot(projected.T, inputs_wide, precision=HIGHEST_PRECISION) + jnp.dot(warm_start, error_sum.T, precision=HIGHEST_PRECISION)
        basis_rows = orthonormal(factor)
        mapped = jnp.dot(inputs_wide, basis_rows.T, precision=HIGHEST_PRECISION)
        second = jnp.dot(mapped.T, grads_wide, precision=HIGHEST_PRECISION) + jnp.dot(basis_rows, error_sum, precision=HIGHEST_PRECISION)
        second = second / math.sqrt(TOKENS * D)
        passed_list.insert(0, passed)
        basis_list.insert(0, basis_rows)
        right_list.insert(0, second)
        arriving = passed
    return (jnp.stack(passed_list), jnp.stack(basis_list), jnp.stack(right_list))
```

```python
import functools
import math

import jax
import jax.numpy as jnp
from jax import lax
from jax.experimental import pallas as pl
from jax.experimental.pallas import tpu as pltpu
from jax.sharding import PartitionSpec as P

MICRO = 4
CORES = 2
HIGHEST = lax.Precision.HIGHEST
VMEM = pl.BlockSpec(memory_space=pltpu.VMEM)


def gather_weights(w_out, w_value):
    replicas = lax.axis_size("dp")
    chips = replicas // CORES
    rank = lax.axis_index("dp")
    chip, core = rank // CORES, rank % CORES
    rows, channels = w_out.shape
    chunk = rows * CORES

    def swap(value, first=0, last=chips):
        pairs = [(i, i ^ 1) for i in range(first * CORES, last * CORES)]
        return lax.ppermute(value, "dp", pairs)

    got = swap(jnp.where(core == 0, w_value, w_out))
    own = jnp.where(
        core == 0, jnp.concatenate([w_out, got], 0), jnp.concatenate([got, w_value], 0)
    )
    whole = jnp.zeros((CORES, replicas * rows + chunk, channels), w_out.dtype)

    def put(whole, piece, kind, place):
        return lax.dynamic_update_slice(whole, piece[None], (kind, place * chunk, 0))

    whole = put(whole, own, core, chip)
    whole = put(whole, swap(own), 1 - core, chip)
    up = down = own
    for step in range(1, chips):
        up_pairs = [(i - CORES, i) for i in range(step * CORES, replicas)]
        down_pairs = [(i + CORES, i) for i in range(0, replicas - step * CORES)]
        up, down = lax.ppermute(up, "dp", up_pairs), lax.ppermute(down, "dp", down_pairs)
        for piece, first, last, source in (
            (up, step, chips, chip - step),
            (down, 0, chips - step, chip + step),
        ):
            place = jnp.where((source >= 0) & (source < chips), source, chips)
            whole = put(whole, piece, core, place)
            whole = put(whole, swap(piece, first, last), 1 - core, place)
    return whole


def stage(whole, arriving, gates, value_grads, passed_rows, *, section, part):
    rows, width = arriving.shape
    channels = gates.shape[1]
    pieces = 4
    piece = width // pieces

    def body(w, arr, gate, vg_in, passed_in, vg_ref, passed_ref, send):
        del vg_in, passed_in
        at = pl.ds(part * rows, rows)

        @pl.when(lax.axis_index("section") == section)
        def _():
            hidden = jnp.dot(arr[...], w[0, :width], preferred_element_type=jnp.float32)
            value_grad = (hidden * gate[at].astype(jnp.float32)).astype(jnp.bfloat16)
            vg_ref[at] = value_grad
            for k in range(pieces):
                cols = pl.ds(k * piece, piece)
                back = lax.dot_general(
                    value_grad, w[1, cols], (((1,), (1,)), ((), ())),
                    preferred_element_type=jnp.float32,
                )
                passed = (arr[:, cols].astype(jnp.float32) + back).astype(jnp.bfloat16)
                passed_ref[at, cols] = passed
                send[:, cols] = passed

    return pl.pallas_call(
        body,
        in_specs=[VMEM] * 5,
        out_specs=[VMEM] * 3,
        out_shape=[
            jax.ShapeDtypeStruct(value_grads.shape, value_grads.dtype),
            jax.ShapeDtypeStruct(passed_rows.shape, passed_rows.dtype),
            jax.ShapeDtypeStruct(arriving.shape, arriving.dtype),
        ],
        input_output_aliases={3: 0, 4: 1},
        compiler_params=pltpu.CompilerParams(vmem_limit_bytes=8 << 20),
        cost_estimate=pl.CostEstimate(
            flops=4 * rows * width * channels, bytes_accessed=4 * width * channels, transcendentals=0
        ),
        name=f"stage_{section}_{part}",
    )(whole, arriving, gates, value_grads, passed_rows)


def split3(value):
    high = value.astype(jnp.bfloat16)
    rest = value - high.astype(jnp.float32)
    middle = rest.astype(jnp.bfloat16)
    low = (rest - middle.astype(jnp.float32)).astype(jnp.bfloat16)
    return jnp.concatenate([high, middle, low], 0)


def join3(value):
    count = value.shape[0] // 3
    return value[:count] + (value[count : 2 * count] + value[2 * count :])


def orthonormal(vectors):
    result = []
    for column in range(vectors.shape[0]):
        current = vectors[column : column + 1]
        for previous in result:
            current = current - jnp.mean(current * previous, axis=1, keepdims=True) * previous
        mean = jnp.mean(current * current, axis=1, keepdims=True)
        result.append(current / jnp.sqrt(mean + 1e-06))
    return jnp.concatenate(result, 0)


def second_half(left, right, inputs, value_grads, error):
    def body(left, right, acts, vg, err, basis_ref, second_ref):
        basis = orthonormal(left[...] + right[...])
        basis_ref[...] = basis
        parts = split3(basis)
        mapped = lax.dot_general(
            parts, acts[...], (((1,), (1,)), ((), ())), preferred_element_type=jnp.float32
        )
        second = jnp.dot(parts, err[...], preferred_element_type=jnp.float32)
        second = second + jnp.dot(
            split3(join3(mapped)), vg[...], preferred_element_type=jnp.float32
        )
        second_ref[...] = join3(second)

    rank, width = left.shape
    channels = value_grads.shape[1]
    return pl.pallas_call(
        body,
        in_specs=[VMEM] * 5,
        out_specs=[VMEM] * 2,
        out_shape=[
            jax.ShapeDtypeStruct((rank, width), jnp.float32),
            jax.ShapeDtypeStruct((rank, channels), jnp.float32),
        ],
        compiler_params=pltpu.CompilerParams(vmem_limit_bytes=8 << 20),
        name="second_half",
    )(left, right, inputs, value_grads, error)


def exchange(value, by):
    replicas = lax.axis_size("dp")
    return lax.ppermute(value, "dp", [(i, i ^ by) for i in range(replicas)])


def sum_but_last(value):
    by = 1
    while by * 2 < lax.axis_size("dp"):
        value = value + exchange(value, by)
        by *= 2
    return value, exchange(value, by)


def local(acts, gates, w_value, w_out, residual_error, grad_top, warm_factor):
    sections = lax.axis_size("section")
    replicas = lax.axis_size("dp")
    inputs, gate_rows, error, warm = acts[0], gates[0], residual_error[0], warm_factor[0]
    row_count, width = inputs.shape
    block = row_count // MICRO
    error_part = lax.dot_general(
        warm, error.astype(jnp.float32), (((1,), (1,)), ((), ())), precision=HIGHEST
    )
    whole = gather_weights(w_out[0], w_value[0])
    value_grads = jnp.zeros((row_count, gate_rows.shape[1]), jnp.bfloat16)
    passed_rows = jnp.zeros((row_count, width), jnp.bfloat16)
    arriving = [grad_top[k * block : (k + 1) * block] for k in range(MICRO)]
    for section in reversed(range(sections)):
        for k in range(MICRO):
            value_grads, passed_rows, send = stage(
                whole, arriving[k], gate_rows, value_grads, passed_rows, section=section, part=k
            )
            if section:
                arriving[k] = lax.ppermute(send, "section", [(section, section - 1)])
    projected = jnp.dot(value_grads.astype(jnp.float32), warm.T, precision=HIGHEST)
    factor = lax.dot_general(
        projected, inputs.astype(jnp.float32), (((0,), (0,)), ((), ())), precision=HIGHEST
    )
    left, right = sum_but_last(factor + error_part)
    basis, second = second_half(left, right, inputs, value_grads, error)
    left, right = sum_but_last(second)
    right_out = (left + right) / math.sqrt(row_count * replicas * width)
    return passed_rows[None], basis[None], right_out[None]


def solution(mesh):
    return jax.shard_map(
        local,
        mesh=mesh,
        in_specs=(
            P("section", "dp", None),
            P("section", "dp", None),
            P("section", "dp", None),
            P("section", "dp", None),
            P("section", "dp", None),
            P("dp", None),
            P("section", None, None),
        ),
        out_specs=(P("section", "dp", None), P("section", None, None), P("section", None, None)),
        check_vma=False,
    )
```

```python
import math

import jax
import jax.numpy as jnp
from jax import lax
from jax.experimental import pallas as pl
from jax.experimental.pallas import tpu as pltpu
from jax.sharding import PartitionSpec as P


MICRO = 4
CORES = 2
HIGHEST = lax.Precision.HIGHEST
VMEM = pl.BlockSpec(memory_space=pltpu.VMEM)
ANY = pl.BlockSpec(memory_space=pl.ANY)


def put(whole, pieces, shape, dtype):
    arrays = list({id(piece): piece for _, piece, _, _ in pieces}.values())
    rows = arrays[0].shape[0]
    if rows % 16:
        whole = jnp.zeros(shape, dtype) if whole is None else whole
        rank = lax.axis_index("dp")
        for kind, piece, source, valid in pieces:
            at = jnp.clip(source(rank), 0, shape[1] // rows - 1) * rows
            held = lax.dynamic_slice(whole, (kind, at, 0), (1,) + piece.shape)
            piece = jnp.where(valid(rank), piece[None], held)
            whole = lax.dynamic_update_slice(whole, piece, (kind, at, 0))
        return whole

    def body(*refs):
        out, done = refs[-2:]
        rank = lax.axis_index("dp")
        for phase in ("start", "wait"):
            for sem, (kind, piece, source, valid) in enumerate(pieces):
                ref = refs[[array is piece for array in arrays].index(True)]

                @pl.when(valid(rank))
                def _():
                    at = pl.ds(pl.multiple_of(source(rank) * rows, 16), rows)
                    copy = pltpu.make_async_copy(ref, out.at[kind, at], done.at[sem])
                    getattr(copy, phase)()

    held = [] if whole is None else [whole]
    return pl.pallas_call(
        body,
        in_specs=[ANY] * len(arrays) + [VMEM] * len(held),
        out_specs=VMEM,
        out_shape=jax.ShapeDtypeStruct(shape, dtype),
        input_output_aliases={len(arrays): 0} if held else {},
        scratch_shapes=[pltpu.SemaphoreType.DMA((len(pieces),))],
        compiler_params=pltpu.CompilerParams(vmem_limit_bytes=4 << 20),
        name="put",
    )(*arrays, *held)


def gather_weights(matrices):
    sections = lax.axis_size("section")
    replicas = lax.axis_size("dp")
    chips = replicas // CORES
    top = sections - 1
    relayed = top > 0 and chips > 3
    rows, channels = matrices[0].shape
    shape, dtype = (len(matrices), replicas * rows, channels), matrices[0].dtype

    def permute(value, moves):
        pairs = [
            ((s * chips + c) * CORES + k, (t * chips + d) * CORES + k)
            for s, c, t, d in moves
            for k in range(CORES)
        ]
        return lax.ppermute(value, ("section", "dp"), pairs)

    def line(value, moves, skip=()):
        moves = [(s, c, s, d) for s in range(sections) for c, d in moves]
        return permute(value, [move for move in moves if move not in skip])

    def swap(value, first=0, last=chips):
        pairs = [(i, i ^ 1) for i in range(first * CORES, last * CORES)]
        return lax.ppermute(value, "dp", pairs)

    def shards(piece, other, by, first=0, last=chips, at_top=None):
        def source(rank):
            return rank + by * CORES

        def beside(rank):
            return rank + by * CORES + 1 - 2 * (rank % CORES)

        def valid(rank):
            inside = (rank >= first * CORES) & (rank < last * CORES)
            if at_top is not None:
                inside &= (lax.axis_index("section") == top) == at_top
            return inside

        return [(piece, source, valid), (other, beside, valid)]

    inner, outer = (1, chips - 2), (0, chips - 1)
    dropped = [(top, c, top, d) for c, d in zip(inner, outer)] if relayed else []
    up, down = list(matrices), list(matrices)
    relay = None
    groups = [[], [], []]
    for step in range(1, chips):
        for kind in range(len(matrices)):
            skip = dropped if step == 1 and kind == 1 else ()
            if step < chips - 1:
                moves = [(c - 1, c) for c in range(step, chips)]
                up[kind] = line(up[kind], moves, skip)
                moves = [(c + 1, c) for c in range(chips - step)]
                down[kind] = line(down[kind], moves, skip)
            else:
                low = lax.axis_index("dp") < replicas // 2
                last = jnp.where(low, down[kind], up[kind])
                moves = [(1, 0), (chips - 2, chips - 1)]
                up[kind] = line(last, moves)
        if step == 1:
            if relayed:
                relay = permute(matrices[1], [(top, c, 0, c) for c in inner])
                relay = permute(relay, [(0, c, 0, d) for c, d in zip(inner, outer)])
                relay = permute(relay, [(0, c, top, c) for c in outer])
            for kind, matrix in enumerate(matrices):
                own = shards(matrix, swap(matrix), 0)
                groups[0] += [(kind,) + piece for piece in own]
        for kind in range(len(matrices)):
            if step < chips - 1:
                from_below = swap(up[kind], step, chips)
                from_above = swap(down[kind], 0, chips - step)
                low, high = (1, chips - 1) if step == 1 and kind == 1 and relayed else (0, chips)
                pieces = shards(up[kind], from_below, -step, step, high)
                pieces += shards(down[kind], from_above, step, low, chips - step)
                if low:
                    pieces += shards(up[kind], from_below, -step, high, chips, False)
                    pieces += shards(down[kind], from_above, step, 0, low, False)
            else:
                other = swap(up[kind])
                pieces = shards(up[kind], other, step, 0, 1)
                pieces += shards(up[kind], other, -step, step, chips)
            behind = 2 * (chips - 1 - step) + len(matrices) - 1 - kind
            groups[0 if behind > 3 else 1 if behind else 2] += [
                (kind,) + piece for piece in pieces
            ]
        if relayed and step == chips - 2:
            other = swap(relay)
            pieces = shards(relay, other, 1, 0, 1, True)
            pieces += shards(relay, other, -1, chips - 1, chips, True)
            groups[1] += [(1,) + piece for piece in pieces]
    whole = None
    for group in groups:
        whole = put(whole, group, shape, dtype)
    return whole


def stage(whole, arriving, gates, held, early, *, section, part, block):
    width = arriving.shape[1]
    row_count, channels = gates.shape
    lanes, deep = math.gcd(channels, 256), math.gcd(width, 512)
    at = pl.ds(part * block, block)
    read = at if arriving.shape[0] == row_count else pl.ds(0, block)

    def body(w, arr, gate, *refs):
        vg_ref, passed_ref, send = refs[-3:]

        @pl.when(lax.axis_index("section") == section)
        def _():
            def forward(step, carry):
                cols = pl.ds(pl.multiple_of(step * lanes, lanes), lanes)
                hidden = jnp.dot(
                    arr[read], w[0, :width, cols], preferred_element_type=jnp.float32
                )
                hidden = hidden * gate[at, cols].astype(jnp.float32)
                vg_ref[at, cols] = hidden.astype(jnp.bfloat16)
                return carry

            lax.fori_loop(0, channels // lanes, forward, 0)

            def backward(step, carry):
                cols = pl.ds(pl.multiple_of(step * deep, deep), deep)
                back = lax.dot_general(
                    vg_ref[at], w[1, cols], (((1,), (1,)), ((), ())),
                    preferred_element_type=jnp.float32,
                )
                passed = (arr[read, cols].astype(jnp.float32) + back).astype(jnp.bfloat16)
                passed_ref[at, cols] = passed
                send[:, cols] = passed
                return carry

            lax.fori_loop(0, width // deep, backward, 0)

    return pl.pallas_call(
        body,
        in_specs=[VMEM] * 3 + [ANY] + [VMEM] * len(held),
        out_specs=[VMEM] * 3,
        out_shape=[
            jax.ShapeDtypeStruct((row_count, channels), jnp.bfloat16),
            jax.ShapeDtypeStruct((row_count, width), jnp.bfloat16),
            jax.ShapeDtypeStruct((block, width), jnp.bfloat16),
        ],
        input_output_aliases={4 + k: k for k in range(len(held))},
        compiler_params=pltpu.CompilerParams(vmem_limit_bytes=8 << 20),
        cost_estimate=pl.CostEstimate(
            flops=4 * block * width * channels,
            bytes_accessed=4 * width * channels,
            transcendentals=0,
        ),
    )(whole, arriving, gates, early, *held)


def split3(value):
    high = value.astype(jnp.bfloat16)
    rest = value - high.astype(jnp.float32)
    middle = rest.astype(jnp.bfloat16)
    low = (rest - middle.astype(jnp.float32)).astype(jnp.bfloat16)
    return jnp.concatenate([high, middle, low], 0)


def join3(value):
    count = value.shape[0] // 3
    return value[:count] + (value[count : 2 * count] + value[2 * count :])


def orthonormal(vectors):
    result = []
    for column in range(vectors.shape[0]):
        current = vectors[column : column + 1]
        for previous in result:
            current = current - jnp.mean(current * previous, axis=1, keepdims=True) * previous
        mean = jnp.mean(current * current, axis=1, keepdims=True)
        result.append(current / jnp.sqrt(mean + 1e-06))
    return jnp.concatenate(result, 0)


def second_half(left, right, inputs, value_grads, error, passed_rows):
    def body(left, right, acts, vg, err, passed, basis_ref, second_ref, out_ref, done):
        copy = pltpu.make_async_copy(passed, out_ref, done)
        copy.start()
        basis = orthonormal(left[...] + right[...])
        basis_ref[...] = basis
        parts = split3(basis)
        mapped = lax.dot_general(
            parts, acts[...], (((1,), (1,)), ((), ())), preferred_element_type=jnp.float32
        )
        second = jnp.dot(parts, err[...], preferred_element_type=jnp.float32)
        second = second + jnp.dot(
            split3(join3(mapped)), vg[...], preferred_element_type=jnp.float32
        )
        second_ref[...] = join3(second)
        copy.wait()

    rank, width = left.shape
    channels = value_grads.shape[1]
    return pl.pallas_call(
        body,
        in_specs=[VMEM] * 6,
        out_specs=[VMEM, VMEM, ANY],
        out_shape=[
            jax.ShapeDtypeStruct((rank, width), jnp.float32),
            jax.ShapeDtypeStruct((rank, channels), jnp.float32),
            jax.ShapeDtypeStruct(passed_rows.shape, passed_rows.dtype),
        ],
        scratch_shapes=[pltpu.SemaphoreType.DMA],
        compiler_params=pltpu.CompilerParams(vmem_limit_bytes=8 << 20),
        name="second_half",
    )(left, right, inputs, value_grads, error, passed_rows)


def exchange(value, by):
    replicas = lax.axis_size("dp")
    return lax.ppermute(value, "dp", [(i, i ^ by) for i in range(replicas)])


def sum_but_last(value):
    by = 1
    while by * 2 < lax.axis_size("dp"):
        value = value + exchange(value, by)
        by *= 2
    return value, exchange(value, by)


def local(acts, gates, w_value, w_out, residual_error, grad_top, warm_factor):
    sections = lax.axis_size("section")
    replicas = lax.axis_size("dp")
    inputs, gate_rows, error, warm = acts[0], gates[0], residual_error[0], warm_factor[0]
    row_count, width = inputs.shape
    error_part = lax.dot_general(
        warm, error.astype(jnp.float32), (((1,), (1,)), ((), ())), precision=HIGHEST
    )
    whole = gather_weights((w_out[0], w_value[0]))
    arriving = [grad_top] * MICRO
    held = []
    for section in reversed(range(sections)):
        for k in range(MICRO):
            *held, send = stage(
                whole, arriving[k], gate_rows, held, error_part,
                section=section, part=k, block=row_count // MICRO,
            )
            if section:
                arriving[k] = lax.ppermute(send, "section", [(section, section - 1)])
    value_grads, passed_rows = held
    projected = jnp.dot(value_grads.astype(jnp.float32), warm.T, precision=HIGHEST)
    factor = lax.dot_general(
        projected, inputs.astype(jnp.float32), (((0,), (0,)), ((), ())), precision=HIGHEST
    )
    left, right = sum_but_last(factor + error_part)
    basis, second, grad_in = second_half(left, right, inputs, value_grads, error, passed_rows)
    left, right = sum_but_last(second)
    right_out = (left + right) / math.sqrt(row_count * replicas * width)
    return grad_in[None], basis[None], right_out[None]


def solution(mesh):
    return jax.shard_map(
        local,
        mesh=mesh,
        in_specs=(
            P("section", "dp", None),
            P("section", "dp", None),
            P("section", "dp", None),
            P("section", "dp", None),
            P("section", "dp", None),
            P("dp", None),
            P("section", None, None),
        ),
        out_specs=(P("section", "dp", None), P("section", None, None), P("section", None, None)),
        check_vma=False,
    )
```

```python
import math

import jax
import jax.numpy as jnp
from jax import lax
from jax.experimental import pallas as pl
from jax.experimental.pallas import tpu as pltpu
from jax.sharding import PartitionSpec as P


SIXTEENTHS = (3, 3, 3, 3, 4)
CORES = 2
HIGHEST = lax.Precision.HIGHEST
VMEM = pl.BlockSpec(memory_space=pltpu.VMEM)
ANY = pl.BlockSpec(memory_space=pl.ANY)


def put(whole, pieces, shape, dtype, after=()):
    arrays = list({id(piece): piece for _, piece, _, _ in pieces}.values())
    rows = arrays[0].shape[0]
    if rows % 16:
        whole = jnp.zeros(shape, dtype) if whole is None else whole
        rank = lax.axis_index("dp")
        for kind, piece, source, valid in pieces:
            at = jnp.clip(source(rank), 0, shape[1] // rows - 1) * rows
            held = lax.dynamic_slice(whole, (kind, at, 0), (1,) + piece.shape)
            piece = jnp.where(valid(rank), piece[None], held)
            whole = lax.dynamic_update_slice(whole, piece, (kind, at, 0))
        return whole

    def body(*refs):
        out, done = refs[-2:]
        rank = lax.axis_index("dp")
        for phase in ("start", "wait"):
            for sem, (kind, piece, source, valid) in enumerate(pieces):
                ref = refs[[array is piece for array in arrays].index(True)]

                @pl.when(valid(rank))
                def _():
                    at = pl.ds(pl.multiple_of(source(rank) * rows, 16), rows)
                    copy = pltpu.make_async_copy(ref, out.at[kind, at], done.at[sem])
                    getattr(copy, phase)()

    held = [] if whole is None else [whole]
    return pl.pallas_call(
        body,
        in_specs=[ANY] * (len(arrays) + len(after)) + [VMEM] * len(held),
        out_specs=VMEM,
        out_shape=jax.ShapeDtypeStruct(shape, dtype),
        input_output_aliases={len(arrays) + len(after): 0} if held else {},
        scratch_shapes=[pltpu.SemaphoreType.DMA((len(pieces),))],
        compiler_params=pltpu.CompilerParams(vmem_limit_bytes=4 << 20),
        name="put",
    )(*arrays, *after, *held)


def gather_weights(matrices):
    sections = lax.axis_size("section")
    replicas = lax.axis_size("dp")
    chips = replicas // CORES
    top = sections - 1
    relayed = top > 0 and chips > 3
    rows, channels = matrices[0].shape
    shape, dtype = (len(matrices), replicas * rows, channels), matrices[0].dtype

    def permute(value, moves):
        pairs = [
            ((s * chips + c) * CORES + k, (t * chips + d) * CORES + k)
            for s, c, t, d in moves
            for k in range(CORES)
        ]
        return lax.ppermute(value, ("section", "dp"), pairs)

    def line(value, moves, skip=()):
        moves = [(s, c, s, d) for s in range(sections) for c, d in moves]
        return permute(value, [move for move in moves if move not in skip])

    def swap(value, first=0, last=chips):
        pairs = [(i, i ^ 1) for i in range(first * CORES, last * CORES)]
        return lax.ppermute(value, "dp", pairs)

    def shards(piece, other, by, first=0, last=chips, at_top=None):
        def source(rank):
            return rank + by * CORES

        def beside(rank):
            return rank + by * CORES + 1 - 2 * (rank % CORES)

        def valid(rank):
            inside = (rank >= first * CORES) & (rank < last * CORES)
            if at_top is not None:
                inside &= (lax.axis_index("section") == top) == at_top
            return inside

        return [(piece, source, valid), (other, beside, valid)]

    inner, outer = (1, chips - 2), (0, chips - 1)
    dropped = [(top, c, top, d) for c, d in zip(inner, outer)] if relayed else []
    up, down = list(matrices), list(matrices)
    relay = None
    groups = [[], [], []]
    for step in range(1, chips):
        for kind in range(len(matrices)):
            skip = dropped if step == 1 and kind == 1 else ()
            if step < chips - 1:
                moves = [(c - 1, c) for c in range(step, chips)]
                up[kind] = line(up[kind], moves, skip)
                moves = [(c + 1, c) for c in range(chips - step)]
                down[kind] = line(down[kind], moves, skip)
            else:
                low = lax.axis_index("dp") < replicas // 2
                last = jnp.where(low, down[kind], up[kind])
                moves = [(1, 0), (chips - 2, chips - 1)]
                split = kind == 1 and top > 0
                skip = [(s, c, s, d) for s in range(top) for c, d in moves] if split else ()
                up[kind] = line(last, moves, skip)
                if split:
                    late = permute(last, skip)
        if step == 1:
            if relayed:
                relay = permute(matrices[1], [(top, c, 0, c) for c in inner])
                relay = permute(relay, [(0, c, 0, d) for c, d in zip(inner, outer)])
                relay = permute(relay, [(0, c, top, c) for c in outer])
            for kind, matrix in enumerate(matrices):
                own = shards(matrix, swap(matrix), 0)
                groups[0] += [(kind,) + piece for piece in own]
        for kind in range(len(matrices)):
            if step < chips - 1:
                from_below = swap(up[kind], step, chips)
                from_above = swap(down[kind], 0, chips - step)
                low, high = (1, chips - 1) if step == 1 and kind == 1 and relayed else (0, chips)
                pieces = shards(up[kind], from_below, -step, step, high)
                pieces += shards(down[kind], from_above, step, low, chips - step)
                if low:
                    pieces += shards(up[kind], from_below, -step, high, chips, False)
                    pieces += shards(down[kind], from_above, step, 0, low, False)
            else:
                other = swap(up[kind])
                whose = True if kind == 1 and top else None
                pieces = shards(up[kind], other, step, 0, 1, whose)
                pieces += shards(up[kind], other, -step, step, chips, whose)
            behind = 2 * (chips - 1 - step) + len(matrices) - 1 - kind
            groups[0 if behind > 3 else 1 if behind else 2] += [
                (kind,) + piece for piece in pieces
            ]
        if relayed and step == chips - 2:
            other = swap(relay)
            pieces = shards(relay, other, 1, 0, 1, True)
            pieces += shards(relay, other, -1, chips - 1, chips, True)
            groups[1] += [(1,) + piece for piece in pieces]
    whole = None
    for group in groups:
        whole = put(whole, group, shape, dtype)

    def finish(whole, after):
        if not top:
            return whole
        other = swap(late)
        pieces = shards(late, other, chips - 1, 0, 1, False)
        pieces += shards(late, other, 1 - chips, chips - 1, chips, False)
        return put(whole, [(1,) + piece for piece in pieces], shape, dtype, after)

    return whole, finish


def stage(whole, arriving, gates, held, early, *, section, first, block):
    width = arriving.shape[1]
    row_count, channels = gates.shape
    lanes, deep = math.gcd(channels, 256), math.gcd(width, 512)
    at = pl.ds(first, block)
    read = at if arriving.shape[0] == row_count else pl.ds(0, block)

    def body(w, arr, gate, *refs):
        vg_ref, passed_ref, send = refs[-3:]

        @pl.when(lax.axis_index("section") == section)
        def _():
            def forward(step, carry):
                cols = pl.ds(pl.multiple_of(step * lanes, lanes), lanes)
                hidden = jnp.dot(
                    arr[read], w[0, :width, cols], preferred_element_type=jnp.float32
                )
                hidden = hidden * gate[at, cols].astype(jnp.float32)
                vg_ref[at, cols] = hidden.astype(jnp.bfloat16)
                return carry

            lax.fori_loop(0, channels // lanes, forward, 0)

            def backward(step, carry):
                cols = pl.ds(pl.multiple_of(step * deep, deep), deep)
                back = lax.dot_general(
                    vg_ref[at], w[1, cols], (((1,), (1,)), ((), ())),
                    preferred_element_type=jnp.float32,
                )
                passed = (arr[read, cols].astype(jnp.float32) + back).astype(jnp.bfloat16)
                passed_ref[at, cols] = passed
                send[:, cols] = passed
                return carry

            lax.fori_loop(0, width // deep, backward, 0)

    return pl.pallas_call(
        body,
        in_specs=[VMEM] * 3 + [ANY] + [VMEM] * len(held),
        out_specs=[VMEM] * 3,
        out_shape=[
            jax.ShapeDtypeStruct((row_count, channels), jnp.bfloat16),
            jax.ShapeDtypeStruct((row_count, width), jnp.bfloat16),
            jax.ShapeDtypeStruct((block, width), jnp.bfloat16),
        ],
        input_output_aliases={4 + k: k for k in range(len(held))},
        compiler_params=pltpu.CompilerParams(vmem_limit_bytes=8 << 20),
        cost_estimate=pl.CostEstimate(
            flops=4 * block * width * channels,
            bytes_accessed=4 * width * channels,
            transcendentals=0,
        ),
    )(whole, arriving, gates, early, *held)


def split3(value):
    high = value.astype(jnp.bfloat16)
    rest = value - high.astype(jnp.float32)
    middle = rest.astype(jnp.bfloat16)
    low = (rest - middle.astype(jnp.float32)).astype(jnp.bfloat16)
    return jnp.concatenate([high, middle, low], 0)


def join3(value):
    count = value.shape[0] // 3
    return value[:count] + (value[count : 2 * count] + value[2 * count :])


def orthonormal(vectors):
    result = []
    for column in range(vectors.shape[0]):
        current = vectors[column : column + 1]
        for previous in result:
            current = current - jnp.mean(current * previous, axis=1, keepdims=True) * previous
        mean = jnp.mean(current * current, axis=1, keepdims=True)
        result.append(current / jnp.sqrt(mean + 1e-06))
    return jnp.concatenate(result, 0)


def second_half(left, right, inputs, value_grads, error, passed_rows):
    def body(left, right, acts, vg, err, passed, basis_ref, second_ref, out_ref, done):
        copy = pltpu.make_async_copy(passed, out_ref, done)
        copy.start()
        basis = orthonormal(left[...] + right[...])
        basis_ref[...] = basis
        parts = split3(basis)
        mapped = lax.dot_general(
            parts, acts[...], (((1,), (1,)), ((), ())), preferred_element_type=jnp.float32
        )
        second = jnp.dot(parts, err[...], preferred_element_type=jnp.float32)
        second = second + jnp.dot(
            split3(join3(mapped)), vg[...], preferred_element_type=jnp.float32
        )
        second_ref[...] = join3(second)
        copy.wait()

    rank, width = left.shape
    channels = value_grads.shape[1]
    return pl.pallas_call(
        body,
        in_specs=[VMEM] * 6,
        out_specs=[VMEM, VMEM, ANY],
        out_shape=[
            jax.ShapeDtypeStruct((rank, width), jnp.float32),
            jax.ShapeDtypeStruct((rank, channels), jnp.float32),
            jax.ShapeDtypeStruct(passed_rows.shape, passed_rows.dtype),
        ],
        scratch_shapes=[pltpu.SemaphoreType.DMA],
        compiler_params=pltpu.CompilerParams(vmem_limit_bytes=8 << 20),
        name="second_half",
    )(left, right, inputs, value_grads, error, passed_rows)


def exchange(value, by):
    replicas = lax.axis_size("dp")
    return lax.ppermute(value, "dp", [(i, i ^ by) for i in range(replicas)])


def sum_but_last(value):
    by = 1
    while by * 2 < lax.axis_size("dp"):
        value = value + exchange(value, by)
        by *= 2
    return value, exchange(value, by)


def local(acts, gates, w_value, w_out, residual_error, grad_top, warm_factor):
    sections = lax.axis_size("section")
    replicas = lax.axis_size("dp")
    inputs, gate_rows, error, warm = acts[0], gates[0], residual_error[0], warm_factor[0]
    row_count, width = inputs.shape
    error_part = lax.dot_general(
        warm, error.astype(jnp.float32), (((1,), (1,)), ((), ())), precision=HIGHEST
    )
    whole, finish = gather_weights((w_out[0], w_value[0]))
    blocks = [count * row_count // 16 for count in SIXTEENTHS]
    firsts = [sum(blocks[:k]) for k in range(len(blocks))]
    arriving = [grad_top] * len(blocks)
    held = []
    for section in reversed(range(sections)):
        for k, (first, block) in enumerate(zip(firsts, blocks)):
            *held, send = stage(
                whole, arriving[k], gate_rows, held, error_part,
                section=section, first=first, block=block,
            )
            if section:
                arriving[k] = lax.ppermute(send, "section", [(section, section - 1)])
        if section == sections - 1:
            whole = finish(whole, held[:1])
    value_grads, passed_rows = held
    projected = jnp.dot(value_grads.astype(jnp.float32), warm.T, precision=HIGHEST)
    factor = lax.dot_general(
        projected, inputs.astype(jnp.float32), (((0,), (0,)), ((), ())), precision=HIGHEST
    )
    left, right = sum_but_last(factor + error_part)
    basis, second, grad_in = second_half(left, right, inputs, value_grads, error, passed_rows)
    left, right = sum_but_last(second)
    right_out = (left + right) / math.sqrt(row_count * replicas * width)
    return grad_in[None], basis[None], right_out[None]


def solution(mesh):
    return jax.shard_map(
        local,
        mesh=mesh,
        in_specs=(
            P("section", "dp", None),
            P("section", "dp", None),
            P("section", "dp", None),
            P("section", "dp", None),
            P("section", "dp", None),
            P("dp", None),
            P("section", None, None),
        ),
        out_specs=(P("section", "dp", None), P("section", None, None), P("section", None, None)),
        check_vma=False,
    )
```

```python
import math

import jax
import jax.numpy as jnp
from jax import lax
from jax.experimental import pallas as pl
from jax.experimental.pallas import tpu as pltpu
from jax.sharding import PartitionSpec as P


SIXTEENTHS = (3, 3, 3, 3, 4)
CORES = 2
HIGHEST = lax.Precision.HIGHEST
VMEM = pl.BlockSpec(memory_space=pltpu.VMEM)
ANY = pl.BlockSpec(memory_space=pl.ANY)


def put(whole, pieces, shape, dtype, after=()):
    arrays = list({id(piece): piece for _, piece, _, _ in pieces}.values())
    rows = arrays[0].shape[-2]
    if rows % 16:
        whole = jnp.zeros(shape, dtype) if whole is None else whole
        rank = lax.axis_index("dp")
        for kind, piece, source, valid in pieces:
            piece = piece[kind] if piece.ndim == 3 else piece
            at = jnp.clip(source(rank), 0, shape[1] // rows - 1) * rows
            held = lax.dynamic_slice(whole, (kind, at, 0), (1,) + piece.shape)
            piece = jnp.where(valid(rank), piece[None], held)
            whole = lax.dynamic_update_slice(whole, piece, (kind, at, 0))
        return whole

    def body(*refs):
        out, done = refs[-2:]
        rank = lax.axis_index("dp")
        for phase in ("start", "wait"):
            for sem, (kind, piece, source, valid) in enumerate(pieces):
                ref = refs[[array is piece for array in arrays].index(True)]

                @pl.when(valid(rank))
                def _():
                    at = pl.ds(pl.multiple_of(source(rank) * rows, 16), rows)
                    part = ref.at[kind] if len(ref.shape) == 3 else ref
                    copy = pltpu.make_async_copy(part, out.at[kind, at], done.at[sem])
                    getattr(copy, phase)()

    held = [] if whole is None else [whole]
    return pl.pallas_call(
        body,
        in_specs=[ANY] * (len(arrays) + len(after)) + [VMEM] * len(held),
        out_specs=VMEM,
        out_shape=jax.ShapeDtypeStruct(shape, dtype),
        input_output_aliases={len(arrays) + len(after): 0} if held else {},
        scratch_shapes=[pltpu.SemaphoreType.DMA((len(pieces),))],
        compiler_params=pltpu.CompilerParams(vmem_limit_bytes=4 << 20),
        name="put",
    )(*arrays, *after, *held)


def gather_weights(matrices):
    sections = lax.axis_size("section")
    replicas = lax.axis_size("dp")
    chips = replicas // CORES
    top = sections - 1
    relayed = top > 0 and chips > 3
    rows, channels = matrices[0].shape
    shape, dtype = (len(matrices), replicas * rows, channels), matrices[0].dtype

    def permute(value, moves):
        pairs = [
            ((s * chips + c) * CORES + k, (t * chips + d) * CORES + k)
            for s, c, t, d in moves
            for k in range(CORES)
        ]
        return lax.ppermute(value, ("section", "dp"), pairs)

    def line(value, moves, skip=()):
        moves = [(s, c, s, d) for s in range(sections) for c, d in moves]
        return permute(value, [move for move in moves if move not in skip])

    def swap(value):
        pairs = [(i, i ^ 1) for i in range(replicas)]
        return lax.ppermute(value, "dp", pairs)

    def shards(piece, other, by, first=0, last=chips, at_top=None):
        def source(rank):
            return rank + by * CORES

        def beside(rank):
            return rank + by * CORES + 1 - 2 * (rank % CORES)

        def valid(rank):
            inside = (rank >= first * CORES) & (rank < last * CORES)
            if at_top is not None:
                inside &= (lax.axis_index("section") == top) == at_top
            return inside

        return [(piece, source, valid), (other, beside, valid)]

    inner, outer = (1, chips - 2), (0, chips - 1)
    dropped = [(top, c, top, d) for c, d in zip(inner, outer)] if relayed else []
    up, down = list(matrices), list(matrices)
    relay = None
    groups = [[], [], []]
    for step in range(1, chips):
        for kind in range(len(matrices)):
            skip = dropped if step == 1 and kind == 1 else ()
            if step < chips - 1:
                moves = [(c - 1, c) for c in range(step, chips)]
                up[kind] = line(up[kind], moves, skip)
                moves = [(c + 1, c) for c in range(chips - step)]
                down[kind] = line(down[kind], moves, skip)
            else:
                low = lax.axis_index("dp") < replicas // 2
                last = jnp.where(low, down[kind], up[kind])
                moves = [(1, 0), (chips - 2, chips - 1)]
                split = kind == 1 and top > 0
                skip = [(s, c, s, d) for s in range(top) for c, d in moves] if split else ()
                up[kind] = line(last, moves, skip)
                if split:
                    late = permute(last, skip)
        if step == 1:
            if relayed:
                relay = permute(matrices[1], [(top, c, 0, c) for c in inner])
                relay = permute(relay, [(0, c, 0, d) for c, d in zip(inner, outer)])
                relay = permute(relay, [(0, c, top, c) for c in outer])
            both = swap(jnp.stack(matrices))
            for kind, matrix in enumerate(matrices):
                groups[0] += [(kind,) + piece for piece in shards(matrix, both, 0)]
        for kind in range(len(matrices)):
            if step < chips - 1:
                from_below = swap(up[kind])
                from_above = swap(down[kind])
                low, high = (1, chips - 1) if step == 1 and kind == 1 and relayed else (0, chips)
                pieces = shards(up[kind], from_below, -step, step, high)
                pieces += shards(down[kind], from_above, step, low, chips - step)
                if low:
                    pieces += shards(up[kind], from_below, -step, high, chips, False)
                    pieces += shards(down[kind], from_above, step, 0, low, False)
            else:
                other = swap(up[kind])
                whose = True if kind == 1 and top else None
                pieces = shards(up[kind], other, step, 0, 1, whose)
                pieces += shards(up[kind], other, -step, step, chips, whose)
            behind = 2 * (chips - 1 - step) + len(matrices) - 1 - kind
            groups[0 if behind > 3 else 1 if behind > 1 else 2] += [
                (kind,) + piece for piece in pieces
            ]
        if relayed and step == chips - 2:
            other = swap(relay)
            pieces = shards(relay, other, 1, 0, 1, True)
            pieces += shards(relay, other, -1, chips - 1, chips, True)
            groups[1] += [(1,) + piece for piece in pieces]
    whole = None
    for group in groups:
        whole = put(whole, group, shape, dtype)

    def finish(whole, after):
        if not top:
            return whole
        other = swap(late)
        pieces = shards(late, other, chips - 1, 0, 1, False)
        pieces += shards(late, other, 1 - chips, chips - 1, chips, False)
        return put(whole, [(1,) + piece for piece in pieces], shape, dtype, after)

    return whole, finish


def stage(whole, arriving, gates, held, early, *, section, first, block):
    width = arriving.shape[1]
    row_count, channels = gates.shape
    lanes, deep = math.gcd(channels, 256), math.gcd(width, 512)
    at = pl.ds(first, block)
    read = at if arriving.shape[0] == row_count else pl.ds(0, block)

    def body(w, arr, gate, *refs):
        vg_ref, passed_ref, send = refs[-3:]

        @pl.when(lax.axis_index("section") == section)
        def _():
            def forward(step, carry):
                cols = pl.ds(pl.multiple_of(step * lanes, lanes), lanes)
                hidden = jnp.dot(
                    arr[read], w[0, :width, cols], preferred_element_type=jnp.float32
                )
                hidden = hidden * gate[at, cols].astype(jnp.float32)
                vg_ref[at, cols] = hidden.astype(jnp.bfloat16)
                return carry

            lax.fori_loop(0, channels // lanes, forward, 0)

            def backward(step, carry):
                cols = pl.ds(pl.multiple_of(step * deep, deep), deep)
                back = lax.dot_general(
                    vg_ref[at], w[1, cols], (((1,), (1,)), ((), ())),
                    preferred_element_type=jnp.float32,
                )
                passed = (arr[read, cols].astype(jnp.float32) + back).astype(jnp.bfloat16)
                passed_ref[at, cols] = passed
                send[:, cols] = passed
                return carry

            lax.fori_loop(0, width // deep, backward, 0)

    return pl.pallas_call(
        body,
        in_specs=[VMEM] * 3 + [ANY] + [VMEM] * len(held),
        out_specs=[VMEM] * 3,
        out_shape=[
            jax.ShapeDtypeStruct((row_count, channels), jnp.bfloat16),
            jax.ShapeDtypeStruct((row_count, width), jnp.bfloat16),
            jax.ShapeDtypeStruct((block, width), jnp.bfloat16),
        ],
        input_output_aliases={4 + k: k for k in range(len(held))},
        compiler_params=pltpu.CompilerParams(vmem_limit_bytes=8 << 20),
        cost_estimate=pl.CostEstimate(
            flops=4 * block * width * channels,
            bytes_accessed=4 * width * channels,
            transcendentals=0,
        ),
    )(whole, arriving, gates, early, *held)


def split3(value):
    high = value.astype(jnp.bfloat16)
    rest = value - high.astype(jnp.float32)
    middle = rest.astype(jnp.bfloat16)
    low = (rest - middle.astype(jnp.float32)).astype(jnp.bfloat16)
    return jnp.concatenate([high, middle, low], 0)


def join3(value):
    count = value.shape[0] // 3
    return value[:count] + (value[count : 2 * count] + value[2 * count :])


def orthonormal(vectors):
    result = []
    for column in range(vectors.shape[0]):
        current = vectors[column : column + 1]
        for previous in result:
            current = current - jnp.mean(current * previous, axis=1, keepdims=True) * previous
        mean = jnp.mean(current * current, axis=1, keepdims=True)
        result.append(current / jnp.sqrt(mean + 1e-06))
    return jnp.concatenate(result, 0)


def second_half(left, right, inputs, value_grads, error, passed_rows):
    def body(left, right, acts, vg, err, passed, basis_ref, second_ref, out_ref, done):
        copy = pltpu.make_async_copy(passed, out_ref, done)
        copy.start()
        basis = orthonormal(left[...] + right[...])
        basis_ref[...] = basis
        parts = split3(basis)
        mapped = lax.dot_general(
            parts, acts[...], (((1,), (1,)), ((), ())), preferred_element_type=jnp.float32
        )
        second = jnp.dot(parts, err[...], preferred_element_type=jnp.float32)
        second = second + jnp.dot(
            split3(join3(mapped)), vg[...], preferred_element_type=jnp.float32
        )
        second_ref[...] = join3(second)
        copy.wait()

    rank, width = left.shape
    channels = value_grads.shape[1]
    return pl.pallas_call(
        body,
        in_specs=[VMEM] * 6,
        out_specs=[VMEM, VMEM, ANY],
        out_shape=[
            jax.ShapeDtypeStruct((rank, width), jnp.float32),
            jax.ShapeDtypeStruct((rank, channels), jnp.float32),
            jax.ShapeDtypeStruct(passed_rows.shape, passed_rows.dtype),
        ],
        scratch_shapes=[pltpu.SemaphoreType.DMA],
        compiler_params=pltpu.CompilerParams(vmem_limit_bytes=8 << 20),
        name="second_half",
    )(left, right, inputs, value_grads, error, passed_rows)


def exchange(value, by):
    replicas = lax.axis_size("dp")
    return lax.ppermute(value, "dp", [(i, i ^ by) for i in range(replicas)])


def sum_but_last(value):
    by = 1
    while by * 2 < lax.axis_size("dp"):
        value = value + exchange(value, by)
        by *= 2
    return value, exchange(value, by)


def local(acts, gates, w_value, w_out, residual_error, grad_top, warm_factor):
    sections = lax.axis_size("section")
    replicas = lax.axis_size("dp")
    inputs, gate_rows, error, warm = acts[0], gates[0], residual_error[0], warm_factor[0]
    row_count, width = inputs.shape
    error_part = lax.dot_general(
        warm, error.astype(jnp.float32), (((1,), (1,)), ((), ())), precision=HIGHEST
    )
    whole, finish = gather_weights((w_out[0], w_value[0]))
    blocks = [count * row_count // 16 for count in SIXTEENTHS]
    firsts = [sum(blocks[:k]) for k in range(len(blocks))]
    arriving = [grad_top] * len(blocks)
    held = []
    for section in reversed(range(sections)):
        for k, (first, block) in enumerate(zip(firsts, blocks)):
            *held, send = stage(
                whole, arriving[k], gate_rows, held, error_part,
                section=section, first=first, block=block,
            )
            if section:
                arriving[k] = lax.ppermute(send, "section", [(section, section - 1)])
        if section == sections - 1:
            whole = finish(whole, held[:1])
    value_grads, passed_rows = held
    projected = jnp.dot(value_grads.astype(jnp.float32), warm.T, precision=HIGHEST)
    factor = lax.dot_general(
        projected, inputs.astype(jnp.float32), (((0,), (0,)), ((), ())), precision=HIGHEST
    )
    left, right = sum_but_last(factor + error_part)
    basis, second, grad_in = second_half(left, right, inputs, value_grads, error, passed_rows)
    left, right = sum_but_last(second)
    right_out = (left + right) / math.sqrt(row_count * replicas * width)
    return grad_in[None], basis[None], right_out[None]


def solution(mesh):
    return jax.shard_map(
        local,
        mesh=mesh,
        in_specs=(
            P("section", "dp", None),
            P("section", "dp", None),
            P("section", "dp", None),
            P("section", "dp", None),
            P("section", "dp", None),
            P("dp", None),
            P("section", None, None),
        ),
        out_specs=(P("section", "dp", None), P("section", None, None), P("section", None, None)),
        check_vma=False,
    )
```

```python
import math

import jax
import jax.numpy as jnp
from jax import lax
from jax.experimental import pallas as pl
from jax.experimental.pallas import tpu as pltpu
from jax.sharding import PartitionSpec as P


SIXTEENTHS = (3, 3, 3, 3, 4)
CORES = 2
HIGHEST = lax.Precision.HIGHEST
VMEM = pl.BlockSpec(memory_space=pltpu.VMEM)
ANY = pl.BlockSpec(memory_space=pl.ANY)


def put(whole, pieces, shape, dtype, after=()):
    arrays = list({id(piece): piece for _, piece, _, _ in pieces}.values())
    rows = arrays[0].shape[-2]
    if rows % 16:
        whole = jnp.zeros(shape, dtype) if whole is None else whole
        rank = lax.axis_index("dp")
        for kind, piece, source, valid in pieces:
            piece = piece[kind] if piece.ndim == 3 else piece
            at = jnp.clip(source(rank), 0, shape[1] // rows - 1) * rows
            held = lax.dynamic_slice(whole, (kind, at, 0), (1,) + piece.shape)
            piece = jnp.where(valid(rank), piece[None], held)
            whole = lax.dynamic_update_slice(whole, piece, (kind, at, 0))
        return whole

    def body(*refs):
        out, done = refs[-2:]
        rank = lax.axis_index("dp")
        for phase in ("start", "wait"):
            for sem, (kind, piece, source, valid) in enumerate(pieces):
                ref = refs[[array is piece for array in arrays].index(True)]

                @pl.when(valid(rank))
                def _():
                    at = pl.ds(pl.multiple_of(source(rank) * rows, 16), rows)
                    part = ref.at[kind] if len(ref.shape) == 3 else ref
                    copy = pltpu.make_async_copy(part, out.at[kind, at], done.at[sem])
                    getattr(copy, phase)()

    held = [] if whole is None else [whole]
    return pl.pallas_call(
        body,
        in_specs=[ANY] * (len(arrays) + len(after)) + [VMEM] * len(held),
        out_specs=VMEM,
        out_shape=jax.ShapeDtypeStruct(shape, dtype),
        input_output_aliases={len(arrays) + len(after): 0} if held else {},
        scratch_shapes=[pltpu.SemaphoreType.DMA((len(pieces),))],
        compiler_params=pltpu.CompilerParams(vmem_limit_bytes=4 << 20),
        name="put",
    )(*arrays, *after, *held)


def gather_weights(matrices):
    sections = lax.axis_size("section")
    replicas = lax.axis_size("dp")
    chips = replicas // CORES
    top = sections - 1
    relayed = top > 0 and chips > 3
    rows, channels = matrices[0].shape
    shape, dtype = (len(matrices), replicas * rows, channels), matrices[0].dtype

    def permute(value, moves):
        pairs = [
            ((s * chips + c) * CORES + k, (t * chips + d) * CORES + k)
            for s, c, t, d in moves
            for k in range(CORES)
        ]
        return lax.ppermute(value, ("section", "dp"), pairs)

    def line(value, moves, skip=()):
        moves = [(s, c, s, d) for s in range(sections) for c, d in moves]
        return permute(value, [move for move in moves if move not in skip])

    def swap(value):
        pairs = [(i, i ^ 1) for i in range(replicas)]
        return lax.ppermute(value, "dp", pairs)

    def shards(piece, other, by, first=0, last=chips, at_top=None):
        def source(rank):
            return rank + by * CORES

        def beside(rank):
            return rank + by * CORES + 1 - 2 * (rank % CORES)

        def valid(rank):
            inside = (rank >= first * CORES) & (rank < last * CORES)
            if at_top is not None:
                inside &= (lax.axis_index("section") == top) == at_top
            return inside

        return [(piece, source, valid), (other, beside, valid)]

    inner, outer = (1, chips - 2), (0, chips - 1)
    dropped = [(top, c, top, d) for c, d in zip(inner, outer)] if relayed else []
    up, down = list(matrices), list(matrices)
    relay = None
    groups = [[], [], []]
    for step in range(1, chips):
        for kind in range(len(matrices)):
            skip = dropped if step == 1 and kind == 1 else ()
            if step < chips - 1:
                moves = [(c - 1, c) for c in range(step, chips)]
                up[kind] = line(up[kind], moves, skip)
                moves = [(c + 1, c) for c in range(chips - step)]
                down[kind] = line(down[kind], moves, skip)
            else:
                low = lax.axis_index("dp") < replicas // 2
                last = jnp.where(low, down[kind], up[kind])
                moves = [(1, 0), (chips - 2, chips - 1)]
                split = kind == 1 and top > 0
                skip = [(s, c, s, d) for s in range(top) for c, d in moves] if split else ()
                up[kind] = line(last, moves, skip)
                if split:
                    late = permute(last, skip)
        if step == 1:
            if relayed:
                relay = permute(matrices[1], [(top, c, 0, c) for c in inner])
                relay = permute(relay, [(0, c, 0, d) for c, d in zip(inner, outer)])
                relay = permute(relay, [(0, c, top, c) for c in outer])
            both = swap(jnp.stack(matrices))
            for kind, matrix in enumerate(matrices):
                groups[0] += [(kind,) + piece for piece in shards(matrix, both, 0)]
        for kind in range(len(matrices)):
            if step < chips - 1:
                from_below = swap(up[kind])
                from_above = swap(down[kind])
                low, high = (1, chips - 1) if step == 1 and kind == 1 and relayed else (0, chips)
                pieces = shards(up[kind], from_below, -step, step, high)
                pieces += shards(down[kind], from_above, step, low, chips - step)
                if low:
                    pieces += shards(up[kind], from_below, -step, high, chips, False)
                    pieces += shards(down[kind], from_above, step, 0, low, False)
            else:
                other = swap(up[kind])
                whose = True if kind == 1 and top else None
                pieces = shards(up[kind], other, step, 0, 1, whose)
                pieces += shards(up[kind], other, -step, step, chips, whose)
            behind = 2 * (chips - 1 - step) + len(matrices) - 1 - kind
            groups[0 if behind > 3 else 1 if behind > 1 else 2] += [
                (kind,) + piece for piece in pieces
            ]
        if relayed and step == chips - 2:
            other = swap(relay)
            pieces = shards(relay, other, 1, 0, 1, True)
            pieces += shards(relay, other, -1, chips - 1, chips, True)
            groups[1] += [(1,) + piece for piece in pieces]
    whole = None
    for group in groups:
        whole = put(whole, group, shape, dtype)

    def finish(whole, after):
        if not top:
            return whole
        other = swap(late)
        pieces = shards(late, other, chips - 1, 0, 1, False)
        pieces += shards(late, other, 1 - chips, chips - 1, chips, False)
        return put(whole, [(1,) + piece for piece in pieces], shape, dtype, after)

    return whole, finish


def stage(whole, arriving, gates, held, early, *, section, first, block):
    width = arriving.shape[1]
    row_count, channels = gates.shape
    lanes, deep = math.gcd(channels, 256), math.gcd(width, 512)
    at = pl.ds(first, block)
    read = at if arriving.shape[0] == row_count else pl.ds(0, block)

    results = [(row_count, channels), (row_count, width)]
    if section:
        results.append((block, width))

    def body(w, arr, gate, early, *refs):
        del early
        vg_ref, passed_ref, *send = refs[len(held) :]

        @pl.when(lax.axis_index("section") == section)
        def _():
            def forward(step, carry):
                cols = pl.ds(pl.multiple_of(step * lanes, lanes), lanes)
                hidden = jnp.dot(
                    arr[read], w[0, :width, cols], preferred_element_type=jnp.float32
                )
                hidden = hidden * gate[at, cols].astype(jnp.float32)
                vg_ref[at, cols] = hidden.astype(jnp.bfloat16)
                return carry

            lax.fori_loop(0, channels // lanes, forward, 0)

            def backward(step, carry):
                cols = pl.ds(pl.multiple_of(step * deep, deep), deep)
                back = lax.dot_general(
                    vg_ref[at], w[1, cols], (((1,), (1,)), ((), ())),
                    preferred_element_type=jnp.float32,
                )
                passed = (arr[read, cols].astype(jnp.float32) + back).astype(jnp.bfloat16)
                passed_ref[at, cols] = passed
                for ref in send:
                    ref[:, cols] = passed
                return carry

            lax.fori_loop(0, width // deep, backward, 0)

    return pl.pallas_call(
        body,
        in_specs=[VMEM] * 3 + [ANY] + [VMEM] * len(held),
        out_specs=[VMEM] * len(results),
        out_shape=[jax.ShapeDtypeStruct(shape, jnp.bfloat16) for shape in results],
        input_output_aliases={4 + k: k for k in range(len(held))},
        compiler_params=pltpu.CompilerParams(vmem_limit_bytes=8 << 20),
        cost_estimate=pl.CostEstimate(
            flops=4 * block * width * channels,
            bytes_accessed=4 * width * channels,
            transcendentals=0,
        ),
    )(whole, arriving, gates, early, *held)


def split3(value):
    high = value.astype(jnp.bfloat16)
    rest = value - high.astype(jnp.float32)
    middle = rest.astype(jnp.bfloat16)
    low = (rest - middle.astype(jnp.float32)).astype(jnp.bfloat16)
    return jnp.concatenate([high, middle, low], 0)


def join3(value):
    count = value.shape[0] // 3
    return value[:count] + (value[count : 2 * count] + value[2 * count :])


def orthonormal(vectors):
    result = []
    for column in range(vectors.shape[0]):
        current = vectors[column : column + 1]
        for previous in result:
            current = current - jnp.mean(current * previous, axis=1, keepdims=True) * previous
        mean = jnp.mean(current * current, axis=1, keepdims=True)
        result.append(current / jnp.sqrt(mean + 1e-06))
    return jnp.concatenate(result, 0)


def second_half(left, right, inputs, value_grads, error, passed_rows):
    def body(left, right, acts, vg, err, passed, basis_ref, second_ref, out_ref, done):
        copy = pltpu.make_async_copy(passed, out_ref, done)
        copy.start()
        basis = orthonormal(left[...] + right[...])
        basis_ref[...] = basis
        parts = split3(basis)
        mapped = lax.dot_general(
            parts, acts[...], (((1,), (1,)), ((), ())), preferred_element_type=jnp.float32
        )
        second = jnp.dot(parts, err[...], preferred_element_type=jnp.float32)
        second = second + jnp.dot(
            split3(join3(mapped)), vg[...], preferred_element_type=jnp.float32
        )
        second_ref[...] = join3(second)
        copy.wait()

    rank, width = left.shape
    channels = value_grads.shape[1]
    return pl.pallas_call(
        body,
        in_specs=[VMEM] * 6,
        out_specs=[VMEM, VMEM, ANY],
        out_shape=[
            jax.ShapeDtypeStruct((rank, width), jnp.float32),
            jax.ShapeDtypeStruct((rank, channels), jnp.float32),
            jax.ShapeDtypeStruct(passed_rows.shape, passed_rows.dtype),
        ],
        scratch_shapes=[pltpu.SemaphoreType.DMA],
        compiler_params=pltpu.CompilerParams(vmem_limit_bytes=8 << 20),
        name="second_half",
    )(left, right, inputs, value_grads, error, passed_rows)


def exchange(value, by):
    replicas = lax.axis_size("dp")
    return lax.ppermute(value, "dp", [(i, i ^ by) for i in range(replicas)])


def sum_but_last(value):
    by = 1
    while by * 2 < lax.axis_size("dp"):
        value = value + exchange(value, by)
        by *= 2
    return value, exchange(value, by)


def local(acts, gates, w_value, w_out, residual_error, grad_top, warm_factor):
    sections = lax.axis_size("section")
    replicas = lax.axis_size("dp")
    inputs, gate_rows, error, warm = acts[0], gates[0], residual_error[0], warm_factor[0]
    row_count, width = inputs.shape
    error_part = lax.dot_general(
        warm, error.astype(jnp.float32), (((1,), (1,)), ((), ())), precision=HIGHEST
    )
    whole, finish = gather_weights((w_out[0], w_value[0]))
    blocks = [count * row_count // 16 for count in SIXTEENTHS]
    firsts = [sum(blocks[:k]) for k in range(len(blocks))]
    arriving = [grad_top] * len(blocks)
    held = []
    for section in reversed(range(sections)):
        for k, (first, block) in enumerate(zip(firsts, blocks)):
            held = stage(
                whole, arriving[k], gate_rows, held, error_part,
                section=section, first=first, block=block,
            )
            if section:
                *held, send = held
                arriving[k] = lax.ppermute(send, "section", [(section, section - 1)])
        if section == sections - 1:
            whole = finish(whole, held[:1])
    value_grads, passed_rows = held
    projected = jnp.dot(value_grads.astype(jnp.float32), warm.T, precision=HIGHEST)
    factor = lax.dot_general(
        projected, inputs.astype(jnp.float32), (((0,), (0,)), ((), ())), precision=HIGHEST
    )
    left, right = sum_but_last(factor + error_part)
    basis, second, grad_in = second_half(left, right, inputs, value_grads, error, passed_rows)
    left, right = sum_but_last(second)
    right_out = (left + right) / math.sqrt(row_count * replicas * width)
    return grad_in[None], basis[None], right_out[None]


def solution(mesh):
    return jax.shard_map(
        local,
        mesh=mesh,
        in_specs=(
            P("section", "dp", None),
            P("section", "dp", None),
            P("section", "dp", None),
            P("section", "dp", None),
            P("section", "dp", None),
            P("dp", None),
            P("section", None, None),
        ),
        out_specs=(P("section", "dp", None), P("section", None, None), P("section", None, None)),
        check_vma=False,
    )
```

```python
import math

import jax
import jax.numpy as jnp
from jax import lax
from jax.experimental import pallas as pl
from jax.experimental.pallas import tpu as pltpu
from jax.sharding import PartitionSpec as P


SIXTEENTHS = (4, 4, 4, 4)
CORES = 2
HIGHEST = lax.Precision.HIGHEST
VMEM = pl.BlockSpec(memory_space=pltpu.VMEM)
ANY = pl.BlockSpec(memory_space=pl.ANY)


def put(whole, pieces, shape, dtype, after=()):
    arrays = list({id(piece): piece for _, piece, _, _ in pieces}.values())
    rows = arrays[0].shape[-2]
    if rows % 16:
        whole = jnp.zeros(shape, dtype) if whole is None else whole
        rank = lax.axis_index("dp")
        for kind, piece, source, valid in pieces:
            piece = piece[kind] if piece.ndim == 3 else piece
            at = jnp.clip(source(rank), 0, shape[1] // rows - 1) * rows
            held = lax.dynamic_slice(whole, (kind, at, 0), (1,) + piece.shape)
            piece = jnp.where(valid(rank), piece[None], held)
            whole = lax.dynamic_update_slice(whole, piece, (kind, at, 0))
        return whole

    def body(*refs):
        out, done = refs[-2:]
        rank = lax.axis_index("dp")
        for phase in ("start", "wait"):
            for sem, (kind, piece, source, valid) in enumerate(pieces):
                ref = refs[[array is piece for array in arrays].index(True)]

                @pl.when(valid(rank))
                def _():
                    at = pl.ds(pl.multiple_of(source(rank) * rows, 16), rows)
                    part = ref.at[kind] if len(ref.shape) == 3 else ref
                    copy = pltpu.make_async_copy(part, out.at[kind, at], done.at[sem])
                    getattr(copy, phase)()

    held = [] if whole is None else [whole]
    return pl.pallas_call(
        body,
        in_specs=[ANY] * (len(arrays) + len(after)) + [VMEM] * len(held),
        out_specs=VMEM,
        out_shape=jax.ShapeDtypeStruct(shape, dtype),
        input_output_aliases={len(arrays) + len(after): 0} if held else {},
        scratch_shapes=[pltpu.SemaphoreType.DMA((len(pieces),))],
        compiler_params=pltpu.CompilerParams(vmem_limit_bytes=4 << 20),
        name="put",
    )(*arrays, *after, *held)


def gather_weights(matrices):
    sections = lax.axis_size("section")
    replicas = lax.axis_size("dp")
    chips = replicas // CORES
    top = sections - 1
    relayed = top > 0 and chips > 3
    rows, channels = matrices[0].shape
    shape, dtype = (len(matrices), replicas * rows, channels), matrices[0].dtype

    def permute(value, moves):
        pairs = [
            ((s * chips + c) * CORES + k, (t * chips + d) * CORES + k)
            for s, c, t, d in moves
            for k in range(CORES)
        ]
        return lax.ppermute(value, ("section", "dp"), pairs)

    def line(value, moves, skip=()):
        moves = [(s, c, s, d) for s in range(sections) for c, d in moves]
        return permute(value, [move for move in moves if move not in skip])

    def swap(value):
        pairs = [(i, i ^ 1) for i in range(replicas)]
        return lax.ppermute(value, "dp", pairs)

    def shards(piece, other, by, first=0, last=chips, at_top=None):
        def source(rank):
            return rank + by * CORES

        def beside(rank):
            return rank + by * CORES + 1 - 2 * (rank % CORES)

        def valid(rank):
            inside = (rank >= first * CORES) & (rank < last * CORES)
            if at_top is not None:
                inside &= (lax.axis_index("section") == top) == at_top
            return inside

        return [(piece, source, valid), (other, beside, valid)]

    inner, outer = (1, chips - 2), (0, chips - 1)
    dropped = [(top, c, top, d) for c, d in zip(inner, outer)] if relayed else []
    up, down = list(matrices), list(matrices)
    relay = None
    groups = [[], [], []]
    late = {}
    for step in range(1, chips):
        for kind in range(len(matrices)):
            skip = dropped if step == 1 and kind == 1 else ()
            if step < chips - 1:
                moves = [(c - 1, c) for c in range(step, chips)]
                up[kind] = line(up[kind], moves, skip)
                moves = [(c + 1, c) for c in range(chips - step)]
                down[kind] = line(down[kind], moves, skip)
            else:
                low = lax.axis_index("dp") < replicas // 2
                last = jnp.where(low, down[kind], up[kind])
                moves = [(1, 0), (chips - 2, chips - 1)]
                if kind == 0 or not top:
                    up[kind] = line(last, moves)
                else:
                    turns = {section: "late" for section in range(1, top)}
                    turns |= {0: "last", top: f"{step}_{kind}"}
                    late = {}
                    for turn in dict.fromkeys(reversed(turns.values())):
                        late[turn] = permute(
                            last,
                            [(s, c, s, d) for s in turns if turns[s] == turn for c, d in moves],
                        )
                    up[kind] = late[f"{step}_{kind}"]
        if step == 1:
            if relayed:
                relay = permute(matrices[1], [(top, c, 0, c) for c in inner])
                relay = permute(relay, [(0, c, 0, d) for c, d in zip(inner, outer)])
                relay = permute(relay, [(0, c, top, c) for c in outer])
            both = swap(jnp.stack(matrices))
            for kind, matrix in enumerate(matrices):
                groups[0] += [(kind,) + piece for piece in shards(matrix, both, 0)]
        for kind in range(len(matrices)):
            if step < chips - 1:
                from_below = swap(up[kind])
                from_above = swap(down[kind])
                low, high = (1, chips - 1) if step == 1 and kind == 1 and relayed else (0, chips)
                pieces = shards(up[kind], from_below, -step, step, high)
                pieces += shards(down[kind], from_above, step, low, chips - step)
                if low:
                    pieces += shards(up[kind], from_below, -step, high, chips, False)
                    pieces += shards(down[kind], from_above, step, 0, low, False)
            else:
                other = swap(up[kind])
                whose = True if kind == 1 and top else None
                pieces = shards(up[kind], other, step, 0, 1, whose)
                pieces += shards(up[kind], other, -step, step, chips, whose)
            behind = 2 * (chips - 1 - step) + len(matrices) - 1 - kind
            groups[0 if behind > 3 else 1 if behind > 1 else 2] += [
                (kind,) + piece for piece in pieces
            ]
        if relayed and step == chips - 2:
            other = swap(relay)
            pieces = shards(relay, other, 1, 0, 1, True)
            pieces += shards(relay, other, -1, chips - 1, chips, True)
            groups[1] += [(1,) + piece for piece in pieces]
    whole = None
    for group in groups:
        whole = put(whole, group, shape, dtype)

    def finish(whole, turn, sections, after):
        if turn not in late:
            return whole
        other = swap(late[turn])

        def here(piece):
            kind, array, source, valid = piece

            def both(rank):
                section = lax.axis_index("section")
                return valid(rank) & (section >= sections[0]) & (section < sections[1])

            return kind, array, source, both

        pieces = shards(late[turn], other, chips - 1, 0, 1)
        pieces += shards(late[turn], other, 1 - chips, chips - 1, chips)
        return put(whole, [here((1,) + piece) for piece in pieces], shape, dtype, after)

    return whole, finish


def stage(whole, arriving, gates, held, early, *, section, first, block):
    width = arriving.shape[1]
    row_count, channels = gates.shape
    lanes, deep = channels, width // 2
    at = pl.ds(first, block)
    read = at if arriving.shape[0] == row_count else pl.ds(0, block)

    results = [(row_count, channels), (row_count, width)]
    if section:
        results.append((block, width))

    def body(w, arr, gate, early, *refs):
        del early
        vg_ref, passed_ref, *send = refs[len(held) :]

        @pl.when(lax.axis_index("section") == section)
        def _():
            def forward(step, carry):
                cols = pl.ds(pl.multiple_of(step * lanes, lanes), lanes)
                hidden = jnp.dot(
                    arr[read], w[0, :width, cols], preferred_element_type=jnp.float32
                )
                hidden = hidden * gate[at, cols].astype(jnp.float32)
                vg_ref[at, cols] = hidden.astype(jnp.bfloat16)
                return carry

            lax.fori_loop(0, channels // lanes, forward, 0)

            def backward(step, carry):
                cols = pl.ds(pl.multiple_of(step * deep, deep), deep)
                back = lax.dot_general(
                    vg_ref[at], w[1, cols], (((1,), (1,)), ((), ())),
                    preferred_element_type=jnp.float32,
                )
                passed = (arr[read, cols].astype(jnp.float32) + back).astype(jnp.bfloat16)
                passed_ref[at, cols] = passed
                for ref in send:
                    ref[:, cols] = passed
                return carry

            lax.fori_loop(0, width // deep, backward, 0)

    return pl.pallas_call(
        body,
        in_specs=[VMEM] * 3 + [ANY] + [VMEM] * len(held),
        out_specs=[VMEM] * len(results),
        out_shape=[jax.ShapeDtypeStruct(shape, jnp.bfloat16) for shape in results],
        input_output_aliases={4 + k: k for k in range(len(held))},
        compiler_params=pltpu.CompilerParams(vmem_limit_bytes=8 << 20),
        cost_estimate=pl.CostEstimate(
            flops=4 * block * width * channels,
            bytes_accessed=4 * width * channels,
            transcendentals=0,
        ),
    )(whole, arriving, gates, early, *held)


def split3(value):
    high = value.astype(jnp.bfloat16)
    rest = value - high.astype(jnp.float32)
    middle = rest.astype(jnp.bfloat16)
    low = (rest - middle.astype(jnp.float32)).astype(jnp.bfloat16)
    return jnp.concatenate([high, middle, low], 0)


def join3(value):
    count = value.shape[0] // 3
    return value[:count] + (value[count : 2 * count] + value[2 * count :])


def orthonormal(vectors):
    result = []
    for column in range(vectors.shape[0]):
        current = vectors[column : column + 1]
        for previous in result:
            current = current - jnp.mean(current * previous, axis=1, keepdims=True) * previous
        mean = jnp.mean(current * current, axis=1, keepdims=True)
        result.append(current / jnp.sqrt(mean + 1e-06))
    return jnp.concatenate(result, 0)


def second_half(left, right, inputs, value_grads, error, passed_rows):
    def body(left, right, acts, vg, err, passed, basis_ref, second_ref, out_ref, done):
        copy = pltpu.make_async_copy(passed, out_ref, done)
        copy.start()
        basis = orthonormal(left[...] + right[...])
        basis_ref[...] = basis
        parts = split3(basis)
        mapped = lax.dot_general(
            parts, acts[...], (((1,), (1,)), ((), ())), preferred_element_type=jnp.float32
        )
        second = jnp.dot(parts, err[...], preferred_element_type=jnp.float32)
        second = second + jnp.dot(
            split3(join3(mapped)), vg[...], preferred_element_type=jnp.float32
        )
        second_ref[...] = join3(second)
        copy.wait()

    rank, width = left.shape
    channels = value_grads.shape[1]
    return pl.pallas_call(
        body,
        in_specs=[VMEM] * 6,
        out_specs=[VMEM, VMEM, ANY],
        out_shape=[
            jax.ShapeDtypeStruct((rank, width), jnp.float32),
            jax.ShapeDtypeStruct((rank, channels), jnp.float32),
            jax.ShapeDtypeStruct(passed_rows.shape, passed_rows.dtype),
        ],
        scratch_shapes=[pltpu.SemaphoreType.DMA],
        compiler_params=pltpu.CompilerParams(vmem_limit_bytes=8 << 20),
        name="second_half",
    )(left, right, inputs, value_grads, error, passed_rows)


def exchange(value, by):
    replicas = lax.axis_size("dp")
    return lax.ppermute(value, "dp", [(i, i ^ by) for i in range(replicas)])


def sum_but_last(value):
    by = 1
    while by * 2 < lax.axis_size("dp"):
        value = value + exchange(value, by)
        by *= 2
    return value, exchange(value, by)


def local(acts, gates, w_value, w_out, residual_error, grad_top, warm_factor):
    sections = lax.axis_size("section")
    replicas = lax.axis_size("dp")
    inputs, gate_rows, error, warm = acts[0], gates[0], residual_error[0], warm_factor[0]
    row_count, width = inputs.shape
    error_part = lax.dot_general(
        warm, error.astype(jnp.float32), (((1,), (1,)), ((), ())), precision=HIGHEST
    )
    whole, finish = gather_weights((w_out[0], w_value[0]))
    blocks = [count * row_count // 16 for count in SIXTEENTHS]
    firsts = [sum(blocks[:k]) for k in range(len(blocks))]
    arriving = [grad_top] * len(blocks)
    held = []
    for section in reversed(range(sections)):
        for k, (first, block) in enumerate(zip(firsts, blocks)):
            held = stage(
                whole, arriving[k], gate_rows, held, error_part,
                section=section, first=first, block=block,
            )
            if section:
                *held, send = held
                arriving[k] = lax.ppermute(send, "section", [(section, section - 1)])
        if section == sections - 1:
            whole = finish(whole, "late", (1, section), held[:1])
        if section == min(1, sections - 1):
            whole = finish(whole, "last", (0, 1), held[:1])
    value_grads, passed_rows = held
    projected = jnp.dot(value_grads.astype(jnp.float32), warm.T, precision=HIGHEST)
    factor = lax.dot_general(
        projected, inputs.astype(jnp.float32), (((0,), (0,)), ((), ())), precision=HIGHEST
    )
    left, right = sum_but_last(factor + error_part)
    basis, second, grad_in = second_half(left, right, inputs, value_grads, error, passed_rows)
    left, right = sum_but_last(second)
    right_out = (left + right) / math.sqrt(row_count * replicas * width)
    return grad_in[None], basis[None], right_out[None]


def solution(mesh):
    return jax.shard_map(
        local,
        mesh=mesh,
        in_specs=(
            P("section", "dp", None),
            P("section", "dp", None),
            P("section", "dp", None),
            P("section", "dp", None),
            P("section", "dp", None),
            P("dp", None),
            P("section", None, None),
        ),
        out_specs=(P("section", "dp", None), P("section", None, None), P("section", None, None)),
        check_vma=False,
    )
```

```python
import math

import jax
import jax.numpy as jnp
from jax import lax
from jax.experimental import pallas as pl
from jax.experimental.pallas import tpu as pltpu
from jax.sharding import PartitionSpec as P


SIXTEENTHS = (4, 4, 4, 4)
CORES = 2
HIGHEST = lax.Precision.HIGHEST
VMEM = pl.BlockSpec(memory_space=pltpu.VMEM)
ANY = pl.BlockSpec(memory_space=pl.ANY)


def put(whole, pieces, shape, dtype, after=()):
    arrays = list({id(piece): piece for _, piece, _, _ in pieces}.values())
    rows = arrays[0].shape[-2]
    if rows % 16:
        whole = jnp.zeros(shape, dtype) if whole is None else whole
        rank = lax.axis_index("dp")
        for kind, piece, source, valid in pieces:
            piece = piece[kind] if piece.ndim == 3 else piece
            at = jnp.clip(source(rank), 0, shape[1] // rows - 1) * rows
            held = lax.dynamic_slice(whole, (kind, at, 0), (1,) + piece.shape)
            piece = jnp.where(valid(rank), piece[None], held)
            whole = lax.dynamic_update_slice(whole, piece, (kind, at, 0))
        return whole

    def body(*refs):
        out, done = refs[-2:]
        rank = lax.axis_index("dp")
        for phase in ("start", "wait"):
            for sem, (kind, piece, source, valid) in enumerate(pieces):
                ref = refs[[array is piece for array in arrays].index(True)]

                @pl.when(valid(rank))
                def _():
                    at = pl.ds(pl.multiple_of(source(rank) * rows, 16), rows)
                    part = ref.at[kind] if len(ref.shape) == 3 else ref
                    copy = pltpu.make_async_copy(part, out.at[kind, at], done.at[sem])
                    getattr(copy, phase)()

    held = [] if whole is None else [whole]
    return pl.pallas_call(
        body,
        in_specs=[ANY] * (len(arrays) + len(after)) + [VMEM] * len(held),
        out_specs=VMEM,
        out_shape=jax.ShapeDtypeStruct(shape, dtype),
        input_output_aliases={len(arrays) + len(after): 0} if held else {},
        scratch_shapes=[pltpu.SemaphoreType.DMA((len(pieces),))],
        compiler_params=pltpu.CompilerParams(vmem_limit_bytes=4 << 20),
        name="put",
    )(*arrays, *after, *held)


def gather_weights(matrices):
    sections = lax.axis_size("section")
    replicas = lax.axis_size("dp")
    chips = replicas // CORES
    top = sections - 1
    relayed = top > 0 and chips > 3
    rows, channels = matrices[0].shape
    shape, dtype = (len(matrices), replicas * rows, channels), matrices[0].dtype

    def permute(value, moves):
        pairs = [
            ((s * chips + c) * CORES + k, (t * chips + d) * CORES + k)
            for s, c, t, d in moves
            for k in range(CORES)
        ]
        return lax.ppermute(value, ("section", "dp"), pairs)

    def line(value, moves, skip=()):
        moves = [(s, c, s, d) for s in range(sections) for c, d in moves]
        return permute(value, [move for move in moves if move not in skip])

    def swap(value):
        pairs = [(i, i ^ 1) for i in range(replicas)]
        return lax.ppermute(value, "dp", pairs)

    def shards(piece, other, by, first=0, last=chips, at_top=None):
        def source(rank):
            return rank + by * CORES

        def beside(rank):
            return rank + by * CORES + 1 - 2 * (rank % CORES)

        def valid(rank):
            inside = (rank >= first * CORES) & (rank < last * CORES)
            if at_top is not None:
                inside &= (lax.axis_index("section") == top) == at_top
            return inside

        return [(piece, source, valid), (other, beside, valid)]

    inner, outer = (1, chips - 2), (0, chips - 1)
    dropped = [(top, c, top, d) for c, d in zip(inner, outer)] if relayed else []
    up, down = list(matrices), list(matrices)
    relay = None
    groups = [[], [], []]
    late = {}
    for step in range(1, chips):
        for kind in range(len(matrices)):
            skip = dropped if step == 1 and kind == 1 else ()
            if step < chips - 1:
                moves = [(c - 1, c) for c in range(step, chips)]
                up[kind] = line(up[kind], moves, skip)
                moves = [(c + 1, c) for c in range(chips - step)]
                down[kind] = line(down[kind], moves, skip)
            else:
                low = lax.axis_index("dp") < replicas // 2
                last = jnp.where(low, down[kind], up[kind])
                moves = [(1, 0), (chips - 2, chips - 1)]
                if kind == 0 or not top:
                    up[kind] = line(last, moves)
                else:
                    turns = {section: "late" for section in range(1, top)}
                    turns |= {0: "last", top: f"{step}_{kind}"}
                    late = {}
                    for turn in dict.fromkeys(reversed(turns.values())):
                        late[turn] = permute(
                            last,
                            [(s, c, s, d) for s in turns if turns[s] == turn for c, d in moves],
                        )
                    up[kind] = late[f"{step}_{kind}"]
        if step == 1:
            if relayed:
                relay = permute(matrices[1], [(top, c, 0, c) for c in inner])
                relay = permute(relay, [(0, c, 0, d) for c, d in zip(inner, outer)])
                relay = permute(relay, [(0, c, top, c) for c in outer])
            both = swap(jnp.stack(matrices))
            for kind, matrix in enumerate(matrices):
                groups[0] += [(kind,) + piece for piece in shards(matrix, both, 0)]
        for kind in range(len(matrices)):
            if step < chips - 1:
                from_below = swap(up[kind])
                from_above = swap(down[kind])
                low, high = (1, chips - 1) if step == 1 and kind == 1 and relayed else (0, chips)
                pieces = shards(up[kind], from_below, -step, step, high)
                pieces += shards(down[kind], from_above, step, low, chips - step)
                if low:
                    pieces += shards(up[kind], from_below, -step, high, chips, False)
                    pieces += shards(down[kind], from_above, step, 0, low, False)
            else:
                other = swap(up[kind])
                whose = True if kind == 1 and top else None
                pieces = shards(up[kind], other, step, 0, 1, whose)
                pieces += shards(up[kind], other, -step, step, chips, whose)
            behind = 2 * (chips - 1 - step) + len(matrices) - 1 - kind
            groups[0 if behind > 3 else 1 if behind > 1 else 2] += [
                (kind,) + piece for piece in pieces
            ]
        if relayed and step == chips - 2:
            other = swap(relay)
            pieces = shards(relay, other, 1, 0, 1, True)
            pieces += shards(relay, other, -1, chips - 1, chips, True)
            groups[1] += [(1,) + piece for piece in pieces]
    whole = None
    for group in groups:
        whole = put(whole, group, shape, dtype)

    def finish(whole, turn, sections, after):
        if turn not in late:
            return whole
        other = swap(late[turn])

        def here(piece):
            kind, array, source, valid = piece

            def both(rank):
                section = lax.axis_index("section")
                return valid(rank) & (section >= sections[0]) & (section < sections[1])

            return kind, array, source, both

        pieces = shards(late[turn], other, chips - 1, 0, 1)
        pieces += shards(late[turn], other, 1 - chips, chips - 1, chips)
        return put(whole, [here((1,) + piece) for piece in pieces], shape, dtype, after)

    return whole, finish


def stage(whole, arriving, gates, held, early, *, section, first, block):
    width = arriving.shape[1]
    row_count, channels = gates.shape
    lanes, deep = channels, width // 2
    at = pl.ds(first, block)
    read = at if arriving.shape[0] == row_count else pl.ds(0, block)

    results = [(row_count, channels), (row_count, width)]
    if section:
        results.append((block, width))

    def body(w, arr, gate, early, *refs):
        del early
        vg_ref, passed_ref, *send = refs[len(held) :]

        @pl.when(lax.axis_index("section") == section)
        def _():
            def forward(step, carry):
                cols = pl.ds(pl.multiple_of(step * lanes, lanes), lanes)
                hidden = jnp.dot(
                    arr[read], w[0, :width, cols], preferred_element_type=jnp.float32
                )
                hidden = hidden * gate[at, cols].astype(jnp.float32)
                vg_ref[at, cols] = hidden.astype(jnp.bfloat16)
                return carry

            lax.fori_loop(0, channels // lanes, forward, 0)

            def backward(step, carry):
                cols = pl.ds(pl.multiple_of(step * deep, deep), deep)
                back = lax.dot_general(
                    vg_ref[at], w[1, cols], (((1,), (1,)), ((), ())),
                    preferred_element_type=jnp.float32,
                )
                passed = (arr[read, cols].astype(jnp.float32) + back).astype(jnp.bfloat16)
                passed_ref[at, cols] = passed
                for ref in send:
                    ref[:, cols] = passed
                return carry

            lax.fori_loop(0, width // deep, backward, 0)

    return pl.pallas_call(
        body,
        in_specs=[VMEM] * 3 + [ANY] + [VMEM] * len(held),
        out_specs=[VMEM] * len(results),
        out_shape=[jax.ShapeDtypeStruct(shape, jnp.bfloat16) for shape in results],
        input_output_aliases={4 + k: k for k in range(len(held))},
        compiler_params=pltpu.CompilerParams(vmem_limit_bytes=8 << 20),
        cost_estimate=pl.CostEstimate(
            flops=4 * block * width * channels,
            bytes_accessed=4 * width * channels,
            transcendentals=0,
        ),
    )(whole, arriving, gates, early, *held)


def split3(value):
    high = value.astype(jnp.bfloat16)
    rest = value - high.astype(jnp.float32)
    middle = rest.astype(jnp.bfloat16)
    low = (rest - middle.astype(jnp.float32)).astype(jnp.bfloat16)
    return jnp.concatenate([high, middle, low], 0)


def join3(value):
    count = value.shape[0] // 3
    return value[:count] + (value[count : 2 * count] + value[2 * count :])


def orthonormal(vectors):
    result = []
    for column in range(vectors.shape[0]):
        current = vectors[column : column + 1]
        for previous in result:
            current = current - jnp.mean(current * previous, axis=1, keepdims=True) * previous
        mean = jnp.mean(current * current, axis=1, keepdims=True)
        result.append(current / jnp.sqrt(mean + 1e-06))
    return jnp.concatenate(result, 0)


def second_half(parts, inputs, value_grads, error, passed_rows):
    def body(*refs):
        *parts, acts, vg, err, passed, basis_ref, second_ref, out_ref, done = refs
        copy = pltpu.make_async_copy(passed, out_ref, done)
        copy.start()
        basis = orthonormal(joined(*(part[...] for part in parts)))
        basis_ref[...] = basis
        pieces = split3(basis)
        mapped = lax.dot_general(
            pieces, acts[...], (((1,), (1,)), ((), ())), preferred_element_type=jnp.float32
        )
        second = jnp.dot(pieces, err[...], preferred_element_type=jnp.float32)
        second = second + jnp.dot(
            split3(join3(mapped)), vg[...], preferred_element_type=jnp.float32
        )
        second_ref[...] = join3(second)
        copy.wait()

    rank, width = parts[0].shape
    channels = value_grads.shape[1]
    return pl.pallas_call(
        body,
        in_specs=[VMEM] * (len(parts) + 4),
        out_specs=[VMEM, VMEM, ANY],
        out_shape=[
            jax.ShapeDtypeStruct((rank, width), jnp.float32),
            jax.ShapeDtypeStruct((rank, channels), jnp.float32),
            jax.ShapeDtypeStruct(passed_rows.shape, passed_rows.dtype),
        ],
        scratch_shapes=[pltpu.SemaphoreType.DMA],
        compiler_params=pltpu.CompilerParams(vmem_limit_bytes=8 << 20),
        name="second_half",
    )(*parts, inputs, value_grads, error, passed_rows)


def exchange(value, by):
    replicas = lax.axis_size("dp")
    return lax.ppermute(value, "dp", [(i, i ^ by) for i in range(replicas)])


def sum_parts(value):
    replicas = lax.axis_size("dp")
    by = 1
    while by * 4 < replicas:
        value = value + exchange(value, by)
        by *= 2
    return value, exchange(value, by), exchange(value, 2 * by), exchange(value, 3 * by)


def joined(first, second, third, fourth):
    return (first + second) + (third + fourth)


def local(acts, gates, w_value, w_out, residual_error, grad_top, warm_factor):
    sections = lax.axis_size("section")
    replicas = lax.axis_size("dp")
    inputs, gate_rows, error, warm = acts[0], gates[0], residual_error[0], warm_factor[0]
    row_count, width = inputs.shape
    error_part = lax.dot_general(
        warm, error.astype(jnp.float32), (((1,), (1,)), ((), ())), precision=HIGHEST
    )
    whole, finish = gather_weights((w_out[0], w_value[0]))
    blocks = [count * row_count // 16 for count in SIXTEENTHS]
    firsts = [sum(blocks[:k]) for k in range(len(blocks))]
    arriving = [grad_top] * len(blocks)
    held = []
    for section in reversed(range(sections)):
        for k, (first, block) in enumerate(zip(firsts, blocks)):
            held = stage(
                whole, arriving[k], gate_rows, held, error_part,
                section=section, first=first, block=block,
            )
            if section:
                *held, send = held
                arriving[k] = lax.ppermute(send, "section", [(section, section - 1)])
        if section == sections - 1:
            whole = finish(whole, "late", (1, section), held[:1])
        if section == min(1, sections - 1):
            whole = finish(whole, "last", (0, 1), held[:1])
    value_grads, passed_rows = held
    projected = jnp.dot(value_grads.astype(jnp.float32), warm.T, precision=HIGHEST)
    factor = lax.dot_general(
        projected, inputs.astype(jnp.float32), (((0,), (0,)), ((), ())), precision=HIGHEST
    )
    parts = sum_parts(factor + error_part)
    basis, second, grad_in = second_half(parts, inputs, value_grads, error, passed_rows)
    right_out = joined(*sum_parts(second)) / math.sqrt(row_count * replicas * width)
    return grad_in[None], basis[None], right_out[None]


def solution(mesh):
    return jax.shard_map(
        local,
        mesh=mesh,
        in_specs=(
            P("section", "dp", None),
            P("section", "dp", None),
            P("section", "dp", None),
            P("section", "dp", None),
            P("section", "dp", None),
            P("dp", None),
            P("section", None, None),
        ),
        out_specs=(P("section", "dp", None), P("section", None, None), P("section", None, None)),
        check_vma=False,
    )
```

```python
import math

import jax
import jax.numpy as jnp
from jax import lax
from jax.experimental import pallas as pl
from jax.experimental.pallas import tpu as pltpu
from jax.sharding import PartitionSpec as P


SIXTEENTHS = (4, 4, 4, 4)
CORES = 2
HIGHEST = lax.Precision.HIGHEST
VMEM = pl.BlockSpec(memory_space=pltpu.VMEM)
ANY = pl.BlockSpec(memory_space=pl.ANY)


def put(whole, pieces, shape, dtype, after=()):
    arrays = list({id(piece): piece for _, piece, _, _ in pieces}.values())
    rows = arrays[0].shape[-2]
    if rows % 16:
        whole = jnp.zeros(shape, dtype) if whole is None else whole
        rank = lax.axis_index("dp")
        for kind, piece, source, valid in pieces:
            piece = piece[kind] if piece.ndim == 3 else piece
            at = jnp.clip(source(rank), 0, shape[1] // rows - 1) * rows
            held = lax.dynamic_slice(whole, (kind, at, 0), (1,) + piece.shape)
            piece = jnp.where(valid(rank), piece[None], held)
            whole = lax.dynamic_update_slice(whole, piece, (kind, at, 0))
        return whole

    def body(*refs):
        out, done = refs[-2:]
        rank = lax.axis_index("dp")
        for phase in ("start", "wait"):
            for sem, (kind, piece, source, valid) in enumerate(pieces):
                ref = refs[[array is piece for array in arrays].index(True)]

                @pl.when(valid(rank))
                def _():
                    at = pl.ds(pl.multiple_of(source(rank) * rows, 16), rows)
                    part = ref.at[kind] if len(ref.shape) == 3 else ref
                    copy = pltpu.make_async_copy(part, out.at[kind, at], done.at[sem])
                    getattr(copy, phase)()

    held = [] if whole is None else [whole]
    return pl.pallas_call(
        body,
        in_specs=[ANY] * (len(arrays) + len(after)) + [VMEM] * len(held),
        out_specs=VMEM,
        out_shape=jax.ShapeDtypeStruct(shape, dtype),
        input_output_aliases={len(arrays) + len(after): 0} if held else {},
        scratch_shapes=[pltpu.SemaphoreType.DMA((len(pieces),))],
        compiler_params=pltpu.CompilerParams(vmem_limit_bytes=4 << 20),
        name="put",
    )(*arrays, *after, *held)


def gather_weights(matrices, meanwhile):
    sections = lax.axis_size("section")
    replicas = lax.axis_size("dp")
    chips = replicas // CORES
    top = sections - 1
    relayed = top > 0 and chips > 3
    rows, channels = matrices[0].shape
    shape, dtype = (len(matrices), replicas * rows, channels), matrices[0].dtype

    def permute(value, moves):
        pairs = [
            ((s * chips + c) * CORES + k, (t * chips + d) * CORES + k)
            for s, c, t, d in moves
            for k in range(CORES)
        ]
        return lax.ppermute(value, ("section", "dp"), pairs)

    def line(value, moves, skip=()):
        moves = [(s, c, s, d) for s in range(sections) for c, d in moves]
        return permute(value, [move for move in moves if move not in skip])

    def swap(value):
        pairs = [(i, i ^ 1) for i in range(replicas)]
        return lax.ppermute(value, "dp", pairs)

    def shards(piece, other, by, first=0, last=chips, at_top=None):
        def source(rank):
            return rank + by * CORES

        def beside(rank):
            return rank + by * CORES + 1 - 2 * (rank % CORES)

        def valid(rank):
            inside = (rank >= first * CORES) & (rank < last * CORES)
            if at_top is not None:
                inside &= (lax.axis_index("section") == top) == at_top
            return inside

        return [(piece, source, valid), (other, beside, valid)]

    inner, outer = (1, chips - 2), (0, chips - 1)
    dropped = [(top, c, top, d) for c, d in zip(inner, outer)] if relayed else []
    up, down = list(matrices), list(matrices)
    relay = None
    groups = [[], [], [], []]
    late = {}
    for step in range(1, chips):
        for kind in range(len(matrices)):
            skip = dropped if step == 1 and kind == 1 else ()
            if step < chips - 1:
                moves = [(c - 1, c) for c in range(step, chips)]
                up[kind] = line(up[kind], moves, skip)
                moves = [(c + 1, c) for c in range(chips - step)]
                down[kind] = line(down[kind], moves, skip)
            else:
                low = lax.axis_index("dp") < replicas // 2
                last = jnp.where(low, down[kind], up[kind])
                moves = [(1, 0), (chips - 2, chips - 1)]
                if kind == 0 or not top:
                    up[kind] = line(last, moves)
                else:
                    turns = {section: "late" for section in range(1, top)}
                    turns |= {0: "last", top: f"{step}_{kind}"}
                    late = {}
                    for turn in dict.fromkeys(reversed(turns.values())):
                        late[turn] = permute(
                            last,
                            [(s, c, s, d) for s in turns if turns[s] == turn for c, d in moves],
                        )
                    up[kind] = late[f"{step}_{kind}"]
        if step == 1:
            if relayed:
                relay = permute(matrices[1], [(top, c, 0, c) for c in inner])
                relay = permute(relay, [(0, c, 0, d) for c, d in zip(inner, outer)])
                relay = permute(relay, [(0, c, top, c) for c in outer])
            both = swap(jnp.stack(matrices))
            for kind, matrix in enumerate(matrices):
                groups[0] += [(kind,) + piece for piece in shards(matrix, both, 0)]
        for kind in range(len(matrices)):
            if step < chips - 1:
                from_below = swap(up[kind])
                from_above = swap(down[kind])
                low, high = (1, chips - 1) if step == 1 and kind == 1 and relayed else (0, chips)
                pieces = shards(up[kind], from_below, -step, step, high)
                pieces += shards(down[kind], from_above, step, low, chips - step)
                if low:
                    pieces += shards(up[kind], from_below, -step, high, chips, False)
                    pieces += shards(down[kind], from_above, step, 0, low, False)
            else:
                other = swap(up[kind])
                whose = True if kind == 1 and top else None
                pieces = shards(up[kind], other, step, 0, 1, whose)
                pieces += shards(up[kind], other, -step, step, chips, whose)
            behind = 2 * (chips - 1 - step) + len(matrices) - 1 - kind
            groups[0 if behind > 3 else 1 if behind > 1 else 3 - behind] += [
                (kind,) + piece for piece in pieces
            ]
        if relayed and step == chips - 2:
            other = swap(relay)
            pieces = shards(relay, other, 1, 0, 1, True)
            pieces += shards(relay, other, -1, chips - 1, chips, True)
            groups[1] += [(1,) + piece for piece in pieces]
    whole = None
    for k, group in enumerate(groups):
        if k == len(groups) - 1:
            ready = meanwhile(whole)
        whole = put(whole, group, shape, dtype, ready[:1] if k == len(groups) - 1 else ())

    def finish(whole, turn, sections, after):
        if turn not in late:
            return whole
        other = swap(late[turn])

        def here(piece):
            kind, array, source, valid = piece

            def both(rank):
                section = lax.axis_index("section")
                return valid(rank) & (section >= sections[0]) & (section < sections[1])

            return kind, array, source, both

        pieces = shards(late[turn], other, chips - 1, 0, 1)
        pieces += shards(late[turn], other, 1 - chips, chips - 1, chips)
        return put(whole, [here((1,) + piece) for piece in pieces], shape, dtype, after)

    return whole, ready, finish


def stage(whole, arriving, gates, held, early, *, section, first, block, forward, backward):
    width = arriving.shape[1]
    row_count, channels = gates.shape
    deep = width // 2
    at = pl.ds(first, block)
    read = at if arriving.shape[0] == row_count else pl.ds(0, block)
    results = [(row_count, channels), (row_count, width)]
    if section and backward:
        results.append((block, width))

    def body(w, arr, gate, early, *refs):
        del early
        vg_ref, passed_ref, *send = refs[len(held) :]

        @pl.when(lax.axis_index("section") == section)
        def _():
            if forward:
                hidden = jnp.dot(arr[read], w[0], preferred_element_type=jnp.float32)
                hidden = hidden * gate[at].astype(jnp.float32)
                vg_ref[at] = hidden.astype(jnp.bfloat16)
            if not backward:
                return

            def step(k, carry):
                cols = pl.ds(pl.multiple_of(k * deep, deep), deep)
                back = lax.dot_general(
                    vg_ref[at], w[1, cols], (((1,), (1,)), ((), ())),
                    preferred_element_type=jnp.float32,
                )
                passed = (arr[read, cols].astype(jnp.float32) + back).astype(jnp.bfloat16)
                passed_ref[at, cols] = passed
                for ref in send:
                    ref[:, cols] = passed
                return carry

            lax.fori_loop(0, width // deep, step, 0)

    return pl.pallas_call(
        body,
        in_specs=[VMEM] * 3 + [ANY] + [VMEM] * len(held),
        out_specs=[VMEM] * len(results),
        out_shape=[jax.ShapeDtypeStruct(shape, jnp.bfloat16) for shape in results],
        input_output_aliases={4 + k: k for k in range(len(held))},
        compiler_params=pltpu.CompilerParams(vmem_limit_bytes=8 << 20),
        cost_estimate=pl.CostEstimate(
            flops=2 * (forward + backward) * block * width * channels,
            bytes_accessed=2 * (forward + backward) * width * channels,
            transcendentals=0,
        ),
    )(whole, arriving, gates, early, *held)


def split3(value):
    high = value.astype(jnp.bfloat16)
    rest = value - high.astype(jnp.float32)
    middle = rest.astype(jnp.bfloat16)
    low = (rest - middle.astype(jnp.float32)).astype(jnp.bfloat16)
    return jnp.concatenate([high, middle, low], 0)


def join3(value):
    count = value.shape[0] // 3
    return value[:count] + (value[count : 2 * count] + value[2 * count :])


def orthonormal(vectors):
    result = []
    for column in range(vectors.shape[0]):
        current = vectors[column : column + 1]
        for previous in result:
            current = current - jnp.mean(current * previous, axis=1, keepdims=True) * previous
        mean = jnp.mean(current * current, axis=1, keepdims=True)
        result.append(current / jnp.sqrt(mean + 1e-06))
    return jnp.concatenate(result, 0)


def second_half(parts, inputs, value_grads, error, passed_rows):
    def body(*refs):
        *parts, acts, vg, err, passed, basis_ref, second_ref, out_ref, done = refs
        copy = pltpu.make_async_copy(passed, out_ref, done)
        copy.start()
        basis = orthonormal(joined(*(part[...] for part in parts)))
        basis_ref[...] = basis
        pieces = split3(basis)
        mapped = lax.dot_general(
            pieces, acts[...], (((1,), (1,)), ((), ())), preferred_element_type=jnp.float32
        )
        second = jnp.dot(pieces, err[...], preferred_element_type=jnp.float32)
        second = second + jnp.dot(
            split3(join3(mapped)), vg[...], preferred_element_type=jnp.float32
        )
        second_ref[...] = join3(second)
        copy.wait()

    rank, width = parts[0].shape
    channels = value_grads.shape[1]
    return pl.pallas_call(
        body,
        in_specs=[VMEM] * (len(parts) + 4),
        out_specs=[VMEM, VMEM, ANY],
        out_shape=[
            jax.ShapeDtypeStruct((rank, width), jnp.float32),
            jax.ShapeDtypeStruct((rank, channels), jnp.float32),
            jax.ShapeDtypeStruct(passed_rows.shape, passed_rows.dtype),
        ],
        scratch_shapes=[pltpu.SemaphoreType.DMA],
        compiler_params=pltpu.CompilerParams(vmem_limit_bytes=8 << 20),
        name="second_half",
    )(*parts, inputs, value_grads, error, passed_rows)


def exchange(value, by):
    replicas = lax.axis_size("dp")
    return lax.ppermute(value, "dp", [(i, i ^ by) for i in range(replicas)])


def sum_parts(value, turns):
    replicas = lax.axis_size("dp")
    by = 1
    while by * (2 if turns else 4) < replicas:
        value = value + exchange(value, by)
        by *= 2
    if turns:
        return value, exchange(value, by)
    return value, exchange(value, by), exchange(value, 2 * by), exchange(value, 3 * by)


def joined(first, second, *others):
    return (first + second) + joined(*others) if others else first + second


def local(acts, gates, w_value, w_out, residual_error, grad_top, warm_factor):
    sections = lax.axis_size("section")
    replicas = lax.axis_size("dp")
    inputs, gate_rows, error, warm = acts[0], gates[0], residual_error[0], warm_factor[0]
    row_count, width = inputs.shape
    error_part = lax.dot_general(
        warm, error.astype(jnp.float32), (((1,), (1,)), ((), ())), precision=HIGHEST
    )
    top = sections - 1

    def forward_top(whole):
        return stage(
            whole, grad_top, gate_rows, (), error_part, section=top,
            first=0, block=row_count, forward=True, backward=False,
        )

    whole, held, finish = gather_weights((w_out[0], w_value[0]), forward_top)
    blocks = [count * row_count // 16 for count in SIXTEENTHS]
    firsts = [sum(blocks[:k]) for k in range(len(blocks))]
    arriving = [grad_top] * len(blocks)
    for section in reversed(range(sections)):
        for k, (first, block) in enumerate(zip(firsts, blocks)):
            held = stage(
                whole, arriving[k], gate_rows, held, error_part,
                section=section, first=first, block=block,
                forward=section < top, backward=True,
            )
            if section:
                *held, send = held
                arriving[k] = lax.ppermute(send, "section", [(section, section - 1)])
        if section == top:
            whole = finish(whole, "late", (1, section), held[:1])
        if section == min(1, top):
            whole = finish(whole, "last", (0, 1), held[:1])
    value_grads, passed_rows = held
    projected = jnp.dot(value_grads.astype(jnp.float32), warm.T, precision=HIGHEST)
    factor = lax.dot_general(
        projected, inputs.astype(jnp.float32), (((0,), (0,)), ((), ())), precision=HIGHEST
    )
    parts = sum_parts(factor + error_part, True)
    basis, second, grad_in = second_half(parts, inputs, value_grads, error, passed_rows)
    right_out = joined(*sum_parts(second, False)) / math.sqrt(row_count * replicas * width)
    return grad_in[None], basis[None], right_out[None]


def solution(mesh):
    return jax.shard_map(
        local,
        mesh=mesh,
        in_specs=(
            P("section", "dp", None),
            P("section", "dp", None),
            P("section", "dp", None),
            P("section", "dp", None),
            P("section", "dp", None),
            P("dp", None),
            P("section", None, None),
        ),
        out_specs=(P("section", "dp", None), P("section", None, None), P("section", None, None)),
        check_vma=False,
    )
```

```python
import math

import jax
import jax.numpy as jnp
from jax import lax
from jax.experimental import pallas as pl
from jax.experimental.pallas import tpu as pltpu
from jax.sharding import PartitionSpec as P


SIXTEENTHS = (4, 4, 4, 4)
CORES = 2
HIGHEST = lax.Precision.HIGHEST
VMEM = pl.BlockSpec(memory_space=pltpu.VMEM)
ANY = pl.BlockSpec(memory_space=pl.ANY)


def put(whole, pieces, shape, dtype, after=()):
    arrays = list({id(piece): piece for _, piece, _, _ in pieces}.values())
    rows = arrays[0].shape[-2]
    if rows % 16:
        whole = jnp.zeros(shape, dtype) if whole is None else whole
        rank = lax.axis_index("dp")
        for kind, piece, source, valid in pieces:
            piece = piece[kind] if piece.ndim == 3 else piece
            at = jnp.clip(source(rank), 0, shape[1] // rows - 1) * rows
            held = lax.dynamic_slice(whole, (kind, at, 0), (1,) + piece.shape)
            piece = jnp.where(valid(rank), piece[None], held)
            whole = lax.dynamic_update_slice(whole, piece, (kind, at, 0))
        return whole

    def body(*refs):
        out, done = refs[-2:]
        rank = lax.axis_index("dp")
        for phase in ("start", "wait"):
            for sem, (kind, piece, source, valid) in enumerate(pieces):
                ref = refs[[array is piece for array in arrays].index(True)]

                @pl.when(valid(rank))
                def _():
                    at = pl.ds(pl.multiple_of(source(rank) * rows, 16), rows)
                    part = ref.at[kind] if len(ref.shape) == 3 else ref
                    copy = pltpu.make_async_copy(part, out.at[kind, at], done.at[sem])
                    getattr(copy, phase)()

    held = [] if whole is None else [whole]
    return pl.pallas_call(
        body,
        in_specs=[ANY] * (len(arrays) + len(after)) + [VMEM] * len(held),
        out_specs=VMEM,
        out_shape=jax.ShapeDtypeStruct(shape, dtype),
        input_output_aliases={len(arrays) + len(after): 0} if held else {},
        scratch_shapes=[pltpu.SemaphoreType.DMA((len(pieces),))],
        compiler_params=pltpu.CompilerParams(vmem_limit_bytes=4 << 20),
        name="put",
    )(*arrays, *after, *held)


def gather_weights(matrices, meanwhile):
    sections = lax.axis_size("section")
    replicas = lax.axis_size("dp")
    chips = replicas // CORES
    top = sections - 1
    relayed = top > 0 and chips > 3
    rows, channels = matrices[0].shape
    shape, dtype = (len(matrices), replicas * rows, channels), matrices[0].dtype

    def permute(value, moves):
        pairs = [
            ((s * chips + c) * CORES + k, (t * chips + d) * CORES + k)
            for s, c, t, d in moves
            for k in range(CORES)
        ]
        return lax.ppermute(value, ("section", "dp"), pairs)

    def line(value, moves, skip=()):
        moves = [(s, c, s, d) for s in range(sections) for c, d in moves]
        return permute(value, [move for move in moves if move not in skip])

    def swap(value):
        pairs = [(i, i ^ 1) for i in range(replicas)]
        return lax.ppermute(value, "dp", pairs)

    def shards(piece, other, by, first=0, last=chips, at_top=None):
        def source(rank):
            return rank + by * CORES

        def beside(rank):
            return rank + by * CORES + 1 - 2 * (rank % CORES)

        def valid(rank):
            inside = (rank >= first * CORES) & (rank < last * CORES)
            if at_top is not None:
                inside &= (lax.axis_index("section") == top) == at_top
            return inside

        return [(piece, source, valid), (other, beside, valid)]

    inner, outer = (1, chips - 2), (0, chips - 1)
    dropped = [(top, c, top, d) for c, d in zip(inner, outer)] if relayed else []
    up, down = list(matrices), list(matrices)
    relay = None
    groups = [[], [], [], []]
    late = {}
    for step in range(1, chips):
        for kind in range(len(matrices)):
            skip = dropped if step == 1 and kind == 1 else ()
            if step < chips - 1:
                moves = [(c - 1, c) for c in range(step, chips)]
                up[kind] = line(up[kind], moves, skip)
                moves = [(c + 1, c) for c in range(chips - step)]
                down[kind] = line(down[kind], moves, skip)
            else:
                low = lax.axis_index("dp") < replicas // 2
                last = jnp.where(low, down[kind], up[kind])
                moves = [(1, 0), (chips - 2, chips - 1)]
                if kind == 0 or not top:
                    up[kind] = line(last, moves)
                else:
                    turns = {section: "late" for section in range(1, top)}
                    turns |= {0: "last", top: f"{step}_{kind}"}
                    late = {}
                    for turn in dict.fromkeys(reversed(turns.values())):
                        late[turn] = permute(
                            last,
                            [(s, c, s, d) for s in turns if turns[s] == turn for c, d in moves],
                        )
                    up[kind] = late[f"{step}_{kind}"]
        if step == 1:
            if relayed:
                relay = permute(matrices[1], [(top, c, 0, c) for c in inner])
                relay = permute(relay, [(0, c, 0, d) for c, d in zip(inner, outer)])
                relay = permute(relay, [(0, c, top, c) for c in outer])
            both = swap(jnp.stack(matrices))
            for kind, matrix in enumerate(matrices):
                groups[0] += [(kind,) + piece for piece in shards(matrix, both, 0)]
        for kind in range(len(matrices)):
            if step < chips - 1:
                from_below = swap(up[kind])
                from_above = swap(down[kind])
                low, high = (1, chips - 1) if step == 1 and kind == 1 and relayed else (0, chips)
                pieces = shards(up[kind], from_below, -step, step, high)
                pieces += shards(down[kind], from_above, step, low, chips - step)
                if low:
                    pieces += shards(up[kind], from_below, -step, high, chips, False)
                    pieces += shards(down[kind], from_above, step, 0, low, False)
            else:
                other = swap(up[kind])
                whose = True if kind == 1 and top else None
                pieces = shards(up[kind], other, step, 0, 1, whose)
                pieces += shards(up[kind], other, -step, step, chips, whose)
            behind = 2 * (chips - 1 - step) + len(matrices) - 1 - kind
            groups[0 if behind > 3 else 1 if behind > 1 else 3 - behind] += [
                (kind,) + piece for piece in pieces
            ]
        if relayed and step == chips - 2:
            other = swap(relay)
            pieces = shards(relay, other, 1, 0, 1, True)
            pieces += shards(relay, other, -1, chips - 1, chips, True)
            groups[1] += [(1,) + piece for piece in pieces]
    whole = None
    for k, group in enumerate(groups):
        if k == len(groups) - 1:
            ready = meanwhile(whole)
        whole = put(whole, group, shape, dtype, ready[:1] if k == len(groups) - 1 else ())

    def finish(whole, turn, sections, after):
        if turn not in late:
            return whole
        other = swap(late[turn])

        def here(piece):
            kind, array, source, valid = piece

            def both(rank):
                section = lax.axis_index("section")
                return valid(rank) & (section >= sections[0]) & (section < sections[1])

            return kind, array, source, both

        pieces = shards(late[turn], other, chips - 1, 0, 1)
        pieces += shards(late[turn], other, 1 - chips, chips - 1, chips)
        return put(whole, [here((1,) + piece) for piece in pieces], shape, dtype, after)

    return whole, ready, finish


def stage(whole, arriving, gates, held, early, *, section, first, block, forward, backward):
    width = arriving.shape[1]
    row_count, channels = gates.shape
    deep = width // 2
    at = pl.ds(first, block)
    read = at if arriving.shape[0] == row_count else pl.ds(0, block)
    results = [(row_count, channels), (row_count, width)]
    if section and backward:
        results.append((block, width))

    def body(w, arr, gate, early, *refs):
        del early
        vg_ref, passed_ref, *send = refs[len(held) :]

        @pl.when(lax.axis_index("section") == section)
        def _():
            if forward:
                hidden = jnp.dot(arr[read], w[0], preferred_element_type=jnp.float32)
                hidden = hidden * gate[at].astype(jnp.float32)
                vg_ref[at] = hidden.astype(jnp.bfloat16)
            if not backward:
                return

            def step(k, carry):
                cols = pl.ds(pl.multiple_of(k * deep, deep), deep)
                back = lax.dot_general(
                    vg_ref[at], w[1, cols], (((1,), (1,)), ((), ())),
                    preferred_element_type=jnp.float32,
                )
                passed = (arr[read, cols].astype(jnp.float32) + back).astype(jnp.bfloat16)
                passed_ref[at, cols] = passed
                for ref in send:
                    ref[:, cols] = passed
                return carry

            lax.fori_loop(0, width // deep, step, 0)

    return pl.pallas_call(
        body,
        in_specs=[VMEM] * 3 + [ANY] + [VMEM] * len(held),
        out_specs=[VMEM] * len(results),
        out_shape=[jax.ShapeDtypeStruct(shape, jnp.bfloat16) for shape in results],
        input_output_aliases={4 + k: k for k in range(len(held))},
        compiler_params=pltpu.CompilerParams(vmem_limit_bytes=8 << 20),
        cost_estimate=pl.CostEstimate(
            flops=2 * (forward + backward) * block * width * channels,
            bytes_accessed=2 * (forward + backward) * width * channels,
            transcendentals=0,
        ),
    )(whole, arriving, gates, early, *held)


def split3(value):
    high = value.astype(jnp.bfloat16)
    rest = value - high.astype(jnp.float32)
    middle = rest.astype(jnp.bfloat16)
    low = (rest - middle.astype(jnp.float32)).astype(jnp.bfloat16)
    return jnp.concatenate([high, middle, low], 0)


def join3(value):
    count = value.shape[0] // 3
    return value[:count] + (value[count : 2 * count] + value[2 * count :])


def orthonormal(vectors):
    result = []
    for column in range(vectors.shape[0]):
        current = vectors[column : column + 1]
        for previous in result:
            current = current - jnp.mean(current * previous, axis=1, keepdims=True) * previous
        mean = jnp.mean(current * current, axis=1, keepdims=True)
        result.append(current / jnp.sqrt(mean + 1e-06))
    return jnp.concatenate(result, 0)


def second_half(parts, early, inputs, value_grads, error, passed_rows):
    def body(*refs):
        *parts, acts, vg, err, passed, basis_ref, second_ref, out_ref, done = refs
        copy = pltpu.make_async_copy(passed, out_ref, done)
        copy.start()
        *parts, early = (part[...] for part in parts)
        basis = orthonormal(joined(*parts) + early)
        basis_ref[...] = basis
        pieces = split3(basis)
        mapped = lax.dot_general(
            pieces, acts[...], (((1,), (1,)), ((), ())), preferred_element_type=jnp.float32
        )
        second = jnp.dot(pieces, err[...], preferred_element_type=jnp.float32)
        second = second + jnp.dot(
            split3(join3(mapped)), vg[...], preferred_element_type=jnp.float32
        )
        second_ref[...] = join3(second)
        copy.wait()

    rank, width = parts[0].shape
    channels = value_grads.shape[1]
    return pl.pallas_call(
        body,
        in_specs=[VMEM] * (len(parts) + 5),
        out_specs=[VMEM, VMEM, ANY],
        out_shape=[
            jax.ShapeDtypeStruct((rank, width), jnp.float32),
            jax.ShapeDtypeStruct((rank, channels), jnp.float32),
            jax.ShapeDtypeStruct(passed_rows.shape, passed_rows.dtype),
        ],
        scratch_shapes=[pltpu.SemaphoreType.DMA],
        compiler_params=pltpu.CompilerParams(vmem_limit_bytes=8 << 20),
        name="second_half",
    )(*parts, early, inputs, value_grads, error, passed_rows)


def exchange(value, by):
    replicas = lax.axis_size("dp")
    return lax.ppermute(value, "dp", [(i, i ^ by) for i in range(replicas)])


def sum_parts(value):
    by = 1
    while by * 4 < lax.axis_size("dp"):
        value = value + exchange(value, by)
        by *= 2
    return (value,) + tuple(exchange(value, count * by) for count in (1, 2, 3))


def joined(first, second, *others):
    return (first + second) + joined(*others) if others else first + second


def local(acts, gates, w_value, w_out, residual_error, grad_top, warm_factor):
    sections = lax.axis_size("section")
    replicas = lax.axis_size("dp")
    inputs, gate_rows, error, warm = acts[0], gates[0], residual_error[0], warm_factor[0]
    row_count, width = inputs.shape
    error_part = lax.dot_general(
        warm, error.astype(jnp.float32), (((1,), (1,)), ((), ())), precision=HIGHEST
    )
    top = sections - 1

    def forward_top(whole):
        return stage(
            whole, grad_top, gate_rows, (), error_sum, section=top,
            first=0, block=row_count, forward=True, backward=False,
        )

    error_parts = sum_parts(error_part)
    error_sum = joined(*error_parts)
    whole, held, finish = gather_weights((w_out[0], w_value[0]), forward_top)
    blocks = [count * row_count // 16 for count in SIXTEENTHS]
    firsts = [sum(blocks[:k]) for k in range(len(blocks))]
    arriving = [grad_top] * len(blocks)
    for section in reversed(range(sections)):
        for k, (first, block) in enumerate(zip(firsts, blocks)):
            held = stage(
                whole, arriving[k], gate_rows, held, error_sum,
                section=section, first=first, block=block,
                forward=section < top, backward=True,
            )
            if section:
                *held, send = held
                arriving[k] = lax.ppermute(send, "section", [(section, section - 1)])
        if section == top:
            whole = finish(whole, "late", (1, section), held[:1])
        if section == min(1, top):
            whole = finish(whole, "last", (0, 1), held[:1])
    value_grads, passed_rows = held
    projected = jnp.dot(value_grads.astype(jnp.float32), warm.T, precision=HIGHEST)
    factor = lax.dot_general(
        projected, inputs.astype(jnp.float32), (((0,), (0,)), ((), ())), precision=HIGHEST
    )
    parts = sum_parts(factor)
    basis, second, grad_in = second_half(
        parts, error_sum, inputs, value_grads, error, passed_rows
    )
    right_out = joined(*sum_parts(second)) / math.sqrt(row_count * replicas * width)
    return grad_in[None], basis[None], right_out[None]


def solution(mesh):
    return jax.shard_map(
        local,
        mesh=mesh,
        in_specs=(
            P("section", "dp", None),
            P("section", "dp", None),
            P("section", "dp", None),
            P("section", "dp", None),
            P("section", "dp", None),
            P("dp", None),
            P("section", None, None),
        ),
        out_specs=(P("section", "dp", None), P("section", None, None), P("section", None, None)),
        check_vma=False,
    )
```

```python
import math

import jax
import jax.numpy as jnp
from jax import lax
from jax.experimental import pallas as pl
from jax.experimental.pallas import tpu as pltpu
from jax.sharding import PartitionSpec as P


SIXTEENTHS = (4, 4, 4, 4)
CORES = 2
HIGHEST = lax.Precision.HIGHEST
VMEM = pl.BlockSpec(memory_space=pltpu.VMEM)
ANY = pl.BlockSpec(memory_space=pl.ANY)


def put(whole, pieces, shape, dtype, after=()):
    arrays = list({id(piece): piece for _, piece, _, _ in pieces}.values())
    rows = arrays[0].shape[-2]
    if rows % 16:
        whole = jnp.zeros(shape, dtype) if whole is None else whole
        rank = lax.axis_index("dp")
        for kind, piece, source, valid in pieces:
            piece = piece[kind] if piece.ndim == 3 else piece
            at = jnp.clip(source(rank), 0, shape[1] // rows - 1) * rows
            held = lax.dynamic_slice(whole, (kind, at, 0), (1,) + piece.shape)
            piece = jnp.where(valid(rank), piece[None], held)
            whole = lax.dynamic_update_slice(whole, piece, (kind, at, 0))
        return whole

    def body(*refs):
        out, done = refs[-2:]
        rank = lax.axis_index("dp")
        for phase in ("start", "wait"):
            for sem, (kind, piece, source, valid) in enumerate(pieces):
                ref = refs[[array is piece for array in arrays].index(True)]

                @pl.when(valid(rank))
                def _():
                    at = pl.ds(pl.multiple_of(source(rank) * rows, 16), rows)
                    part = ref.at[kind] if len(ref.shape) == 3 else ref
                    copy = pltpu.make_async_copy(part, out.at[kind, at], done.at[sem])
                    getattr(copy, phase)()

    held = [] if whole is None else [whole]
    return pl.pallas_call(
        body,
        in_specs=[ANY] * (len(arrays) + len(after)) + [VMEM] * len(held),
        out_specs=VMEM,
        out_shape=jax.ShapeDtypeStruct(shape, dtype),
        input_output_aliases={len(arrays) + len(after): 0} if held else {},
        scratch_shapes=[pltpu.SemaphoreType.DMA((len(pieces),))],
        compiler_params=pltpu.CompilerParams(vmem_limit_bytes=4 << 20),
        name="put",
    )(*arrays, *after, *held)


def gather_weights(matrices, meanwhile):
    sections = lax.axis_size("section")
    replicas = lax.axis_size("dp")
    chips = replicas // CORES
    top = sections - 1
    relayed = top > 0 and chips > 3
    rows, channels = matrices[0].shape
    shape, dtype = (len(matrices), replicas * rows, channels), matrices[0].dtype

    def permute(value, moves):
        pairs = [
            ((s * chips + c) * CORES + k, (t * chips + d) * CORES + k)
            for s, c, t, d in moves
            for k in range(CORES)
        ]
        return lax.ppermute(value, ("section", "dp"), pairs)

    def line(value, moves, skip=()):
        moves = [(s, c, s, d) for s in range(sections) for c, d in moves]
        return permute(value, [move for move in moves if move not in skip])

    def swap(value):
        pairs = [(i, i ^ 1) for i in range(replicas)]
        return lax.ppermute(value, "dp", pairs)

    def shards(piece, other, by, first=0, last=chips, at_top=None):
        def source(rank):
            return rank + by * CORES

        def beside(rank):
            return rank + by * CORES + 1 - 2 * (rank % CORES)

        def valid(rank):
            inside = (rank >= first * CORES) & (rank < last * CORES)
            if at_top is not None:
                inside &= (lax.axis_index("section") == top) == at_top
            return inside

        return [(piece, source, valid), (other, beside, valid)]

    inner, outer = (1, chips - 2), (0, chips - 1)
    dropped = [(top, c, top, d) for c, d in zip(inner, outer)] if relayed else []
    up, down = list(matrices), list(matrices)
    relay = None
    groups = [[], [], [], []]
    late = {}
    for step in range(1, chips):
        for kind in range(len(matrices)):
            skip = dropped if step == 1 and kind == 1 else ()
            if step < chips - 1:
                moves = [(c - 1, c) for c in range(step, chips)]
                up[kind] = line(up[kind], moves, skip)
                moves = [(c + 1, c) for c in range(chips - step)]
                down[kind] = line(down[kind], moves, skip)
            else:
                low = lax.axis_index("dp") < replicas // 2
                last = jnp.where(low, down[kind], up[kind])
                moves = [(1, 0), (chips - 2, chips - 1)]
                if kind == 0 or not top:
                    up[kind] = line(last, moves)
                else:
                    turns = {section: "late" for section in range(1, top)}
                    turns |= {0: "last", top: f"{step}_{kind}"}
                    late = {}
                    for turn in dict.fromkeys(reversed(turns.values())):
                        late[turn] = permute(
                            last,
                            [(s, c, s, d) for s in turns if turns[s] == turn for c, d in moves],
                        )
                    up[kind] = late[f"{step}_{kind}"]
        if step == 1:
            if relayed:
                relay = permute(matrices[1], [(top, c, 0, c) for c in inner])
                relay = permute(relay, [(0, c, 0, d) for c, d in zip(inner, outer)])
                relay = permute(relay, [(0, c, top, c) for c in outer])
            both = swap(jnp.stack(matrices))
            for kind, matrix in enumerate(matrices):
                groups[0] += [(kind,) + piece for piece in shards(matrix, both, 0)]
        for kind in range(len(matrices)):
            if step < chips - 1:
                from_below = swap(up[kind])
                from_above = swap(down[kind])
                low, high = (1, chips - 1) if step == 1 and kind == 1 and relayed else (0, chips)
                pieces = shards(up[kind], from_below, -step, step, high)
                pieces += shards(down[kind], from_above, step, low, chips - step)
                if low:
                    pieces += shards(up[kind], from_below, -step, high, chips, False)
                    pieces += shards(down[kind], from_above, step, 0, low, False)
            else:
                other = swap(up[kind])
                whose = True if kind == 1 and top else None
                pieces = shards(up[kind], other, step, 0, 1, whose)
                pieces += shards(up[kind], other, -step, step, chips, whose)
            behind = 2 * (chips - 1 - step) + len(matrices) - 1 - kind
            groups[0 if behind > 3 else 1 if behind > 1 else 3 - behind] += [
                (kind,) + piece for piece in pieces
            ]
        if relayed and step == chips - 2:
            other = swap(relay)
            pieces = shards(relay, other, 1, 0, 1, True)
            pieces += shards(relay, other, -1, chips - 1, chips, True)
            groups[1] += [(1,) + piece for piece in pieces]
    whole = None
    for k, group in enumerate(groups):
        if k == len(groups) - 1:
            ready = meanwhile(whole)
        whole = put(whole, group, shape, dtype, ready[:1] if k == len(groups) - 1 else ())

    def finish(whole, turn, sections, after):
        if turn not in late:
            return whole
        other = swap(late[turn])

        def here(piece):
            kind, array, source, valid = piece

            def both(rank):
                section = lax.axis_index("section")
                return valid(rank) & (section >= sections[0]) & (section < sections[1])

            return kind, array, source, both

        pieces = shards(late[turn], other, chips - 1, 0, 1)
        pieces += shards(late[turn], other, 1 - chips, chips - 1, chips)
        return put(whole, [here((1,) + piece) for piece in pieces], shape, dtype, after)

    return whole, ready, finish


def stage(whole, arriving, gates, held, early, *, section, first, block, forward, backward):
    width = arriving.shape[1]
    row_count, channels = gates.shape
    deep = width // 2 if forward else width
    at = pl.ds(first, block)
    read = at if arriving.shape[0] == row_count else pl.ds(0, block)
    results = [(row_count, channels), (row_count, width)]
    if section and backward:
        results.append((block, width))

    def body(w, arr, gate, early, *refs):
        del early
        vg_ref, passed_ref, *send = refs[len(held) :]

        @pl.when(lax.axis_index("section") == section)
        def _():
            if forward:
                hidden = jnp.dot(arr[read], w[0], preferred_element_type=jnp.float32)
                hidden = hidden * gate[at].astype(jnp.float32)
                vg_ref[at] = hidden.astype(jnp.bfloat16)
            if not backward:
                return

            def step(k, carry):
                cols = pl.ds(pl.multiple_of(k * deep, deep), deep)
                back = lax.dot_general(
                    vg_ref[at], w[1, cols], (((1,), (1,)), ((), ())),
                    preferred_element_type=jnp.float32,
                )
                passed = (arr[read, cols].astype(jnp.float32) + back).astype(jnp.bfloat16)
                passed_ref[at, cols] = passed
                for ref in send:
                    ref[:, cols] = passed
                return carry

            lax.fori_loop(0, width // deep, step, 0)

    return pl.pallas_call(
        body,
        in_specs=[VMEM] * 3 + [ANY] + [VMEM] * len(held),
        out_specs=[VMEM] * len(results),
        out_shape=[jax.ShapeDtypeStruct(shape, jnp.bfloat16) for shape in results],
        input_output_aliases={4 + k: k for k in range(len(held))},
        compiler_params=pltpu.CompilerParams(vmem_limit_bytes=8 << 20),
        cost_estimate=pl.CostEstimate(
            flops=2 * (forward + backward) * block * width * channels,
            bytes_accessed=2 * (forward + backward) * width * channels,
            transcendentals=0,
        ),
    )(whole, arriving, gates, early, *held)


def split3(value):
    high = value.astype(jnp.bfloat16)
    rest = value - high.astype(jnp.float32)
    middle = rest.astype(jnp.bfloat16)
    low = (rest - middle.astype(jnp.float32)).astype(jnp.bfloat16)
    return jnp.concatenate([high, middle, low], 0)


def join3(value):
    count = value.shape[0] // 3
    return value[:count] + (value[count : 2 * count] + value[2 * count :])


def orthonormal(vectors):
    result = []
    for column in range(vectors.shape[0]):
        current = vectors[column : column + 1]
        for previous in result:
            current = current - jnp.mean(current * previous, axis=1, keepdims=True) * previous
        mean = jnp.mean(current * current, axis=1, keepdims=True)
        result.append(current / jnp.sqrt(mean + 1e-06))
    return jnp.concatenate(result, 0)


def second_half(parts, inputs, value_grads, error, passed_rows):
    def body(*refs):
        *parts, acts, vg, err, passed, basis_ref, second_ref, out_ref, done = refs
        copy = pltpu.make_async_copy(passed, out_ref, done)
        copy.start()
        basis = orthonormal(parts[0][...] + parts[1][...])
        basis_ref[...] = basis
        pieces = split3(basis)
        mapped = lax.dot_general(
            pieces, acts[...], (((1,), (1,)), ((), ())), preferred_element_type=jnp.float32
        )
        second = jnp.dot(pieces, err[...], preferred_element_type=jnp.float32)
        second = second + jnp.dot(
            split3(join3(mapped)), vg[...], preferred_element_type=jnp.float32
        )
        second_ref[...] = join3(second)
        copy.wait()

    rank, width = parts[0].shape
    channels = value_grads.shape[1]
    return pl.pallas_call(
        body,
        in_specs=[VMEM] * (len(parts) + 4),
        out_specs=[VMEM, VMEM, ANY],
        out_shape=[
            jax.ShapeDtypeStruct((rank, width), jnp.float32),
            jax.ShapeDtypeStruct((rank, channels), jnp.float32),
            jax.ShapeDtypeStruct(passed_rows.shape, passed_rows.dtype),
        ],
        scratch_shapes=[pltpu.SemaphoreType.DMA],
        compiler_params=pltpu.CompilerParams(vmem_limit_bytes=8 << 20),
        name="second_half",
    )(*parts, inputs, value_grads, error, passed_rows)


def exchange(value, by):
    replicas = lax.axis_size("dp")
    return lax.ppermute(value, "dp", [(i, i ^ by) for i in range(replicas)])


def sum_parts(value):
    by = 1
    while by * 2 < lax.axis_size("dp"):
        value = value + exchange(value, by)
        by *= 2
    return value, exchange(value, by)


def first_half(value_grads, inputs, warm, error_part):
    def body(vg, acts, warm, error, out):
        projected = lax.dot_general(
            split3(warm[...]), vg[...], (((1,), (1,)), ((), ())),
            preferred_element_type=jnp.float32,
        )
        factor = jnp.dot(
            split3(join3(projected)), acts[...], preferred_element_type=jnp.float32
        )
        out[...] = join3(factor) + error[...]

    return pl.pallas_call(
        body,
        in_specs=[VMEM] * 4,
        out_specs=VMEM,
        out_shape=jax.ShapeDtypeStruct(error_part.shape, jnp.float32),
        compiler_params=pltpu.CompilerParams(vmem_limit_bytes=8 << 20),
        name="first_half",
    )(value_grads, inputs, warm, error_part)


def local(acts, gates, w_value, w_out, residual_error, grad_top, warm_factor):
    sections = lax.axis_size("section")
    replicas = lax.axis_size("dp")
    inputs, gate_rows, error, warm = acts[0], gates[0], residual_error[0], warm_factor[0]
    row_count, width = inputs.shape
    error_part = lax.dot_general(
        warm, error.astype(jnp.float32), (((1,), (1,)), ((), ())), precision=HIGHEST
    )
    top = sections - 1

    def forward_top(whole):
        return stage(
            whole, grad_top, gate_rows, (), error_part, section=top,
            first=0, block=row_count, forward=True, backward=False,
        )

    whole, held, finish = gather_weights((w_out[0], w_value[0]), forward_top)
    blocks = [count * row_count // 16 for count in SIXTEENTHS]
    firsts = [sum(blocks[:k]) for k in range(len(blocks))]
    arriving = [grad_top] * len(blocks)
    for section in reversed(range(sections)):
        for k, (first, block) in enumerate(zip(firsts, blocks)):
            held = stage(
                whole, arriving[k], gate_rows, held, error_part,
                section=section, first=first, block=block,
                forward=section < top, backward=True,
            )
            if section:
                *held, send = held
                arriving[k] = lax.ppermute(send, "section", [(section, section - 1)])
        if section == top:
            whole = finish(whole, "late", (1, section), held[:1])
        if section == min(1, top):
            whole = finish(whole, "last", (0, 1), held[:1])
    value_grads, passed_rows = held
    parts = sum_parts(first_half(value_grads, inputs, warm, error_part))
    basis, second, grad_in = second_half(parts, inputs, value_grads, error, passed_rows)
    right_out = sum(sum_parts(second)) / math.sqrt(row_count * replicas * width)
    return grad_in[None], basis[None], right_out[None]


def solution(mesh):
    return jax.shard_map(
        local,
        mesh=mesh,
        in_specs=(
            P("section", "dp", None),
            P("section", "dp", None),
            P("section", "dp", None),
            P("section", "dp", None),
            P("section", "dp", None),
            P("dp", None),
            P("section", None, None),
        ),
        out_specs=(P("section", "dp", None), P("section", None, None), P("section", None, None)),
        check_vma=False,
    )
```
